32 devices in a mesh: band: 8 (over z, core), grid: 4 (over y, x).
Axes of the slice: x: 2, y: 2, z: 4, core: 2. Of those that a mesh axis runs over, the one named last changes fastest.
Arguments:
- orbitals: float32 [8, 128, 128, 128], P('band', 'grid')
- sources: int32 [4], replicated, may hold values from 0 to 7, as said below
Outputs:
- compressed: float32 [8, 128, 128, 128], P(None, 'grid', 'band')
The draws below stay inside these ranges and needn't reach their ends.
Inputs may be any that keep to these rules, and one draw needn't show every extreme that they name: `sources`: 4 distinct orbital indices in some order.
All inputs are finite; a program needn't handle non-finite values.
Results may differ from the reference program's by a relative error of at most 0.0003.
Values sent between devices are 32-bit elements; how exact they have to be, the bound alone decides.
A program may use at most 64 MiB of HBM per device.

```python
import math
import jax
import jax.numpy as jnp
from jax import lax

NX = 128
NY = 128
NZ = 128
ROUNDS = 4
NB = 8


def draw_orbitals(key, part):
    first_key, second_key = jax.random.split(jax.random.fold_in(key, 11))
    shape = (NB, NX, NY, NZ)
    rough = jax.random.normal(first_key, shape, jnp.float32)
    spread = 0.15
    coeffs = jax.random.normal(second_key, (NB, 4), jnp.float32) * spread
    xpos = jnp.arange(NX, dtype=jnp.float32)[:, None, None] * (2.0 * math.pi / NX)
    ypos = jnp.arange(NY, dtype=jnp.float32)[None, :, None] * (2.0 * math.pi / NY)
    zpos = jnp.arange(NZ, dtype=jnp.float32)[None, None, :] * (2.0 * math.pi / NZ)
    ones_field = jnp.ones((NX, NY, NZ), jnp.float32)
    modes = jnp.stack([ones_field, jnp.cos(xpos) + 0.0 * ones_field, jnp.cos(ypos) + 0.0 * ones_field, jnp.cos(xpos + zpos) + 0.0 * ones_field])
    smooth = jnp.einsum('bm,mxyz->bxyz', coeffs, modes)
    return rough + smooth


def draw_sources(key, part):
    first_key, second_key = jax.random.split(jax.random.fold_in(key, 7))
    middle = 1 + jax.random.permutation(first_key, NB - 2)
    chosen = jnp.concatenate([jnp.array([0, NB - 1], jnp.int32), middle[:ROUNDS - 2].astype(jnp.int32)])
    chosen = chosen[:ROUNDS]
    order = jax.random.permutation(second_key, ROUNDS)
    return chosen[order].astype(jnp.int32)


def setup_inputs(seed: int = 0) -> dict:
    seeds = jax.random.split(jax.random.key(seed), 3)
    return {
        "orbitals": draw_orbitals(jax.random.fold_in(seeds[2], 71), 0),
        "sources": draw_sources(jax.random.fold_in(seeds[2], 71), 0),
    }


def squared_waves(length):
    index_values = jnp.arange(length, dtype=jnp.int32)
    signed = jnp.where(index_values < length // 2, index_values, index_values - length)
    waves = signed.astype(jnp.float32) * (2.0 * math.pi / length)
    return waves * waves

def reference(orbitals, sources):
    screen = (4.0 * math.pi / NX) ** 2
    waves = squared_waves(NX)[:, None, None] + squared_waves(NY)[None, :, None] + squared_waves(NZ)[None, None, :]
    kernel = 1.0 / (waves + screen)
    picked = orbitals[sources]

    def one_target(target):
        total = jnp.zeros((NX, NY, NZ), jnp.float32)
        for turn in range(ROUNDS):
            source = picked[turn]
            density = target * source
            spectrum = jnp.fft.fftn(density) * kernel
            potential = jnp.real(jnp.fft.ifftn(spectrum)).astype(jnp.float32)
            total = total + source * potential
        return total
    terms = lax.map(one_target, orbitals, batch_size=8)
    flat_orbitals = orbitals.reshape(NB, NX * NY * NZ)
    flat_terms = terms.reshape(NB, NX * NY * NZ)
    volume = 1.0 / (NX * NY * NZ)
    intersection = jnp.dot(flat_orbitals.astype(jnp.float32), flat_terms.T.astype(jnp.float32), precision=lax.Precision.HIGHEST, preferred_element_type=jnp.float32) * volume
    factor = jnp.linalg.cholesky(intersection)
    solved = lax.linalg.triangular_solve(factor, flat_terms, left_side=True, lower=True)
    return (-solved).reshape(NB, NX, NY, NZ)
```

```python
import functools
import math

import jax
import jax.numpy as jnp
import numpy as np
from jax import lax
from jax.experimental import pallas as pl
from jax.experimental.pallas import tpu as pltpu
from jax.sharding import PartitionSpec as P

highest = lax.Precision.HIGHEST
MESH = pl.DeviceIdType.MESH


def spread_2(block, axis, owner):
    block = jnp.where(lax.axis_index(axis) == owner, block, jnp.zeros_like(block))
    return lax.psum(block, axis)


def cas_table(length):
    index_values = jnp.arange(length, dtype=jnp.int32)
    products = index_values[:, None] * index_values[None, :] % length
    angles = products.astype(jnp.float32) * (2.0 * math.pi / length)
    return jnp.cos(angles) + jnp.sin(angles)


def squared_waves(start, count, length):
    index_values = start + jnp.arange(count, dtype=jnp.int32)
    signed = jnp.where(index_values < length // 2, index_values, index_values - length)
    waves = signed.astype(jnp.float32) * (2.0 * math.pi / length)
    return waves * waves


def general(orbitals, sources):
    band_count, slab_x, full_y, full_z = orbitals.shape
    grid_count = lax.axis_size("grid")
    full_x = slab_x * grid_count
    total_bands = band_count * lax.axis_size("band")
    round_count = sources.shape[0]
    table_x = cas_table(full_x)
    table_y = cas_table(full_y)
    table_z = cas_table(full_z)
    column_y = full_y // grid_count
    start_y = lax.axis_index("grid") * column_y
    waves = (
        squared_waves(0, full_x, full_x)[:, None, None]
        + squared_waves(start_y, column_y, full_y)[None, :, None]
        + squared_waves(0, full_z, full_z)[None, None, :]
    )
    screen = (4.0 * math.pi / full_x) ** 2
    volume = 1.0 / (full_x * full_y * full_z)
    kernel = volume / (waves + screen)

    def plane_transform(field):
        spread = jnp.einsum("bxyz,zk->bxyk", field, table_z, precision=highest)
        return jnp.einsum("bxyk,yj->bxjk", spread, table_y, precision=highest)

    def own_slab(number):
        owner = number // band_count
        local = number % band_count
        return (owner, lax.dynamic_index_in_dim(orbitals, local, 0, keepdims=False))

    def fetch(number):
        owner, slab = own_slab(number)
        return spread_2(slab, "band", owner)

    arrived = [fetch(sources[turn]) for turn in range(round_count)]
    terms = jnp.zeros(orbitals.shape, jnp.float32)
    for turn in range(round_count):
        source = arrived[turn][None]
        spectra = plane_transform(orbitals * source)
        potential_columns = lax.all_to_all(spectra, "grid", split_axis=2, concat_axis=1, tiled=True)
        line_spread = jnp.einsum("bxyz,xa->bayz", potential_columns, table_x, precision=highest)
        line_spread = line_spread * kernel[None]
        filtered = jnp.einsum("bayz,ax->bxyz", line_spread, table_x, precision=highest)
        terms = terms + source * plane_transform(
            lax.all_to_all(filtered, "grid", split_axis=1, concat_axis=2, tiled=True)
        )
    orbital_cols, term_cols = (
        lax.all_to_all(orbitals, "band", split_axis=2, concat_axis=0, tiled=True),
        lax.all_to_all(terms, "band", split_axis=2, concat_axis=0, tiled=True),
    )
    flat_orbitals = orbital_cols.reshape(total_bands, -1)
    flat_terms = term_cols.reshape(total_bands, -1)
    partial_intersection = (
        jnp.dot(flat_orbitals, flat_terms.T, precision=highest, preferred_element_type=jnp.float32)
        * volume
    )
    intersection = lax.psum(partial_intersection, ("band", "grid"))
    factor = jnp.linalg.cholesky(intersection)
    solved = lax.linalg.triangular_solve(factor, flat_terms, left_side=True, lower=True)
    return (-solved).reshape(term_cols.shape)


def parts_of(value):
    high = value.astype(jnp.bfloat16)
    low = (value - high.astype(jnp.float32)).astype(jnp.bfloat16)
    return high, low


def along_rows(left, first, second):
    n = first.shape[0]
    h0, l0 = parts_of(first)
    h1, l1 = parts_of(second)
    right = jnp.concatenate(
        [jnp.concatenate([h0, h1], axis=1), jnp.concatenate([l0, l1], axis=1)], axis=0
    )
    both = jnp.dot(left, right, preferred_element_type=jnp.float32)
    return both[:n] + both[n:]


def along_lanes(rows, right):
    n = rows.shape[1]
    high, low = parts_of(rows)
    both = jnp.dot(
        jnp.concatenate([high, low], axis=1), right, preferred_element_type=jnp.float32
    )
    return both[:, :n] + both[:, n:]


def whole_kernel(
    bands, grids, rounds, chunks, ahead, slack, n, volume,
    sources, orbitals, left_ref, right_ref, waves_ref, out, *scratch,
):
    (own, mate, up, dn, src, fcol, spec, cols, back, terms, tcol, part, sums_b, sums_g, splat,
     in_sem, m_send, m_recv, up_send, up_recv, dn_send, dn_recv, s_send, s_recv,
     o_send, o_recv, f_send, f_recv, b_send, b_recv,
     t_send, t_recv, sb_send, sb_recv, sg_send, sg_recv) = scratch
    b = lax.axis_index("band")
    g = lax.axis_index("grid")
    nz = bands // 2
    z, core = b // 2, b % 2
    slab = n // grids
    depth = slab // chunks
    ycols = n // grids
    piece = ycols * depth
    yb = n // bands
    half = slab // 2
    units = half
    per = depth // 2
    total_units = rounds * units
    lag = (nz - 1) * ahead
    partner = z * 2 + (1 - core)

    barrier = pltpu.get_barrier_semaphore()
    for d in range(1, bands):
        pl.semaphore_signal(barrier, inc=1, device_id=(lax.rem(b + d, bands), g), device_id_type=MESH)
    for d in range(1, grids):
        pl.semaphore_signal(barrier, inc=1, device_id=(b, lax.rem(g + d, grids)), device_id_type=MESH)
    loads = [
        pltpu.make_async_copy(
            orbitals.at[0, pl.ds(h * half, half)], own.at[pl.ds(h * half, half)], in_sem.at[h]
        )
        for h in range(2)
    ]
    for load in loads:
        load.start()
    for load in loads:
        load.wait()
    pl.semaphore_wait(barrier, bands + grids - 2)

    def mate_copy(u):
        return pltpu.make_async_remote_copy(
            src_ref=own.at[2 * u + 1 - core],
            dst_ref=mate.at[u],
            send_sem=m_send.at[u], recv_sem=m_recv.at[u],
            device_id=(partner, g), device_id_type=MESH,
        )

    def up_copy(v):
        return pltpu.make_async_remote_copy(
            src_ref=up.at[v], dst_ref=up.at[v],
            send_sem=up_send.at[v], recv_sem=up_recv.at[v],
            device_id=(lax.rem(b + 2, bands), g), device_id_type=MESH,
        )

    def dn_copy(v):
        return pltpu.make_async_remote_copy(
            src_ref=dn.at[v], dst_ref=dn.at[v],
            send_sem=dn_send.at[v], recv_sem=dn_recv.at[v],
            device_id=(lax.rem(b + bands - 2, bands), g), device_id_type=MESH,
        )

    def src_copy(v, side):
        r, u = lax.div(v, units), lax.rem(v, units)
        block = src.at[r, 2 * u + side]
        return pltpu.make_async_remote_copy(
            src_ref=block, dst_ref=block,
            send_sem=s_send.at[v], recv_sem=s_recv.at[v],
            device_id=(partner, g), device_id_type=MESH,
        )

    def mate_start(u, _):
        mate_copy(u).start()
        return 0

    lax.fori_loop(0, units, mate_start, 0)

    def step(t, _):
        @pl.when(t < units)
        def _():
            mate_copy(t).wait_recv()

        def pass_on(v, box, copy, first, last):
            @pl.when(jnp.logical_and(v >= 0, v < total_units))
            def _():
                r, u = lax.div(v, units), lax.rem(v, units)
                s = sources[r]
                here = jnp.where(
                    s == b, own[2 * u + core], mate[u]
                )

                @pl.when(first)
                def _():
                    box[v] = here

                @pl.when(jnp.logical_not(first))
                def _():
                    copy(v).wait_recv()
                    box[v] = jnp.where(jnp.logical_or(s == b, s == partner), here, box[v])

                @pl.when(jnp.logical_not(last))
                def _():
                    copy(v).start()

        pass_on(t - z * ahead, up, up_copy, z == 0, z == nz - 1)
        pass_on(t - (nz - 1 - z) * ahead, dn, dn_copy, z == nz - 1, z == 0)
        v = t - lag

        @pl.when(jnp.logical_and(v >= 0, v < total_units))
        def _():
            r, u = lax.div(v, units), lax.rem(v, units)
            src[r, 2 * u + core] = jnp.where(
                sources[r] < 2 * z + 2, up[v], dn[v]
            )
            src_copy(v, core).start()

        return 0

    def o_copy(target, owner):
        return pltpu.make_async_remote_copy(
            src_ref=own.at[:, pl.ds(target * yb, yb)], dst_ref=fcol.at[owner],
            send_sem=o_send.at[target], recv_sem=o_recv.at[owner],
            device_id=(target, g), device_id_type=MESH,
        )

    left = left_ref[...]
    right = right_ref[...]

    def f_copy(c, r, target, owner):
        return pltpu.make_async_remote_copy(
            src_ref=spec.at[c * rounds + r, pl.ds(target * piece, piece)],
            dst_ref=cols.at[r, owner * chunks + c],
            send_sem=f_send.at[(c * rounds + r) * grids + target],
            recv_sem=f_recv.at[(c * rounds + r) * grids + owner],
            device_id=(b, target), device_id_type=MESH,
        )

    def b_copy(c, r, target, owner):
        return pltpu.make_async_remote_copy(
            src_ref=cols.at[r, target * chunks + c],
            dst_ref=back.at[c * rounds + r, pl.ds(owner * piece, piece)],
            send_sem=b_send.at[(c * rounds + r) * grids + target],
            recv_sem=b_recv.at[(c * rounds + r) * grids + owner],
            device_id=(b, target), device_id_type=MESH,
        )

    base = waves_ref[...]

    def forward_chunk(c, r):
        for k in range(0, depth, 2):
            at = c * depth + k
            pair = src[r, pl.ds(at, 2)] * own[pl.ds(at, 2)]
            rows = along_lanes(pair.reshape(2 * n, n), right)
            planes = along_rows(left, rows[:n], rows[n:])
            spec[c * rounds + r, pl.ds(k, n, stride=depth), :] = planes[:, :n]
            spec[c * rounds + r, pl.ds(k + 1, n, stride=depth), :] = planes[:, n:]
        for d in range(1, grids):
            f_copy(c, r, lax.rem(g + d, grids), g).start()
        cols[r, g * chunks + c] = spec[c * rounds + r, pl.ds(g * piece, piece), :]

    def forward(r):
        def chunk(c, _):
            first = r * units + c * per
            done = first + lag + slack
            begin = jnp.where(c == 0, 0, done) if r == 0 else done
            lax.fori_loop(begin, done + per, step, 0)
            for e in range(per):
                src_copy(first + e, 1 - core).wait_recv()
            forward_chunk(c, r)
            return 0

        lax.fori_loop(0, chunks, chunk, 0)

    def lines(r):
        for c in range(chunks):
            for d in range(1, grids):
                f_copy(c, r, g, lax.rem(g + d, grids)).wait_recv()

        def line(k, _):
            held = [
                cols[r, :, pl.ds(pl.multiple_of((2 * k + e) * depth, depth), depth), :].reshape(n, n)
                for e in range(2)
            ]
            moved = along_rows(left, held[0], held[1])
            filtered = []
            for e in range(2):
                ky = g * ycols + 2 * k + e
                signed = jnp.where(ky < n // 2, ky, ky - n).astype(jnp.float32)
                wave = signed * (2.0 * math.pi / n)
                filtered.append(moved[:, e * n:(e + 1) * n] * (volume / (base + wave * wave)))
            done = along_rows(left, filtered[0], filtered[1])
            for e in range(2):
                cols[r, :, pl.ds(pl.multiple_of((2 * k + e) * depth, depth), depth), :] = (
                    done[:, e * n:(e + 1) * n].reshape(grids * chunks, depth, n)
                )
            return 0

        lax.fori_loop(0, ycols // 2, line, 0)

    def give_back(c, r):
        for d in range(1, grids):
            b_copy(c, r, lax.rem(g + d, grids), g).start()

    def inverse(c, r):
        for d in range(1, grids):
            b_copy(c, r, g, lax.rem(g + d, grids)).wait_recv()
        back[c * rounds + r, pl.ds(g * piece, piece), :] = cols[r, g * chunks + c]
        for k in range(0, depth, 2):
            planes = along_rows(
                left,
                back[c * rounds + r, pl.ds(k, n, stride=depth), :],
                back[c * rounds + r, pl.ds(k + 1, n, stride=depth), :],
            )
            rows = jnp.concatenate([planes[:, :n], planes[:, n:]], axis=0)
            potential = along_lanes(rows, right).reshape(2, n, n)
            at = c * depth + k
            here = src[r, pl.ds(at, 2)] * potential
            if r == 0:
                terms[pl.ds(at, 2)] = here
            else:
                terms[pl.ds(at, 2)] += here

    def inverse_all(r):
        def one(c, _):
            inverse(c, r)
            return 0

        lax.fori_loop(0, chunks, one, 0)

    tail = min(2, rounds)
    returned = 0
    for r in range(rounds):
        forward(r)
        if r == rounds - 1:
            for d in range(1, bands):
                o_copy(lax.rem(b + d, bands), b).start()
        if r % 2 == 1 and returned < rounds - tail:
            lines(returned)
            for c in range(chunks):
                give_back(c, returned)
            returned += 1
            ready = returned - 1
            if ready > 0:
                inverse_all(ready - 1)
    while returned < rounds - tail:
        lines(returned)
        for c in range(chunks):
            give_back(c, returned)
        returned += 1
        if returned > 1:
            inverse_all(returned - 2)
    for r in range(rounds - tail, rounds):
        lines(r)
    for c in range(chunks):
        for r in range(rounds - tail, rounds):
            give_back(c, r)
    fcol[b] = own[:, pl.ds(b * yb, yb), :]
    if rounds > tail:
        inverse_all(rounds - tail - 1)

    def t_copy(c, target, owner):
        return pltpu.make_async_remote_copy(
            src_ref=terms.at[pl.ds(c * depth, depth), pl.ds(target * yb, yb)],
            dst_ref=tcol.at[owner, pl.ds(c * depth, depth)],
            send_sem=t_send.at[c * bands + target],
            recv_sem=t_recv.at[c * bands + owner],
            device_id=(target, g), device_id_type=MESH,
        )

    def overlap(c):
        for d in range(1, bands):
            t_copy(c, b, lax.rem(b + d, bands)).wait_recv()

        def one(i, _):
            mine = fcol[i, pl.ds(c * depth, depth)]
            for k in range(bands):
                prod = mine * tcol[k, pl.ds(c * depth, depth)]
                total = jnp.sum(prod.reshape(-1, 8, n), axis=0)
                if c == 0:
                    part[i * bands + k] = total
                else:
                    part[i * bands + k] += total
            return 0

        lax.fori_loop(0, bands, one, 0)

    for c in range(chunks):
        for r in range(rounds - tail, rounds):
            inverse(c, r)
        for d in range(1, bands):
            t_copy(c, lax.rem(b + d, bands), b).start()
        tcol[b, pl.ds(c * depth, depth)] = terms[pl.ds(c * depth, depth), pl.ds(b * yb, yb), :]
        if c == 1:
            for d in range(1, bands):
                o_copy(b, lax.rem(b + d, bands)).wait_recv()
        if c > 0:
            overlap(c - 1)
    overlap(chunks - 1)

    count = bands * bands
    flat = jnp.sum(part[...], axis=1)
    if count < n:
        flat = jnp.concatenate([flat, jnp.zeros((n - count, n), jnp.float32)], axis=0)
    lanes = jnp.sum(flat.T, axis=0, keepdims=True)
    sums_b[b] = jnp.broadcast_to(lanes, (8, n))

    def sb_copy(target, owner):
        return pltpu.make_async_remote_copy(
            src_ref=sums_b.at[b], dst_ref=sums_b.at[owner],
            send_sem=sb_send.at[target], recv_sem=sb_recv.at[owner],
            device_id=(target, g), device_id_type=MESH,
        )

    def sg_copy(target, owner):
        return pltpu.make_async_remote_copy(
            src_ref=sums_g.at[g], dst_ref=sums_g.at[owner],
            send_sem=sg_send.at[target], recv_sem=sg_recv.at[owner],
            device_id=(b, target), device_id_type=MESH,
        )

    for d in range(1, bands):
        sb_copy(lax.rem(b + d, bands), b).start()
    for d in range(1, bands):
        sb_copy(b, lax.rem(b + d, bands)).wait_recv()
    sums_g[g] = jnp.sum(sums_b[...], axis=0)
    for d in range(1, grids):
        sg_copy(lax.rem(g + d, grids), g).start()
    for d in range(1, grids):
        sg_copy(g, lax.rem(g + d, grids)).wait_recv()
    total = jnp.sum(sums_g[...], axis=0)[:1] * volume
    splat[...] = jnp.broadcast_to(total, (n, n)).T

    def entry(i, k):
        first = splat[pl.ds(i * bands + k, 1), :]
        return 0.5 * (first + splat[pl.ds(k * bands + i, 1), :])

    factor = {}
    inverse_diag = {}
    for k in range(bands):
        diag = entry(k, k)
        for m in range(k):
            diag = diag - factor[k, m] * factor[k, m]
        inverse_diag[k] = 1.0 / jnp.sqrt(diag)
        for i in range(k + 1, bands):
            value = entry(i, k)
            for m in range(k):
                value = value - factor[i, m] * factor[k, m]
            factor[i, k] = value * inverse_diag[k]
    for k in range(bands):
        splat[pl.ds(k * bands + k, 1), :] = inverse_diag[k]
        for i in range(k + 1, bands):
            splat[pl.ds(i * bands + k, 1), :] = factor[i, k]

    def solve(x, _):
        solved = []
        for i in range(bands):
            value = -tcol[i, x]
            for k in range(i):
                value = value - splat[pl.ds(i * bands + k, 1), :] * solved[k]
            value = value * splat[pl.ds(i * bands + i, 1), :]
            out[i, x] = value
            solved.append(value)
        return 0

    lax.fori_loop(0, slab, solve, 0)

    def mate_settle(u, _):
        mate_copy(u).wait_send()
        return 0

    lax.fori_loop(0, units, mate_settle, 0)

    def settle(v, _):
        @pl.when(z < nz - 1)
        def _():
            up_copy(v).wait_send()

        @pl.when(z > 0)
        def _():
            dn_copy(v).wait_send()

        src_copy(v, core).wait_send()
        return 0

    lax.fori_loop(0, total_units, settle, 0)
    for d in range(1, bands):
        o_copy(lax.rem(b + d, bands), b).wait_send()
    for c in range(chunks):
        for r in range(rounds):
            for d in range(1, grids):
                f_copy(c, r, lax.rem(g + d, grids), g).wait_send()
                b_copy(c, r, lax.rem(g + d, grids), g).wait_send()
        for d in range(1, bands):
            t_copy(c, lax.rem(b + d, bands), b).wait_send()
    for d in range(1, bands):
        sb_copy(lax.rem(b + d, bands), b).wait_send()
    for d in range(1, grids):
        sg_copy(lax.rem(g + d, grids), g).wait_send()


def fused(bands, grids, orbitals, sources):
    n = orbitals.shape[2]
    rounds = sources.shape[0]
    slab = n // grids
    depth = 8
    chunks = slab // depth
    yb = n // bands
    numbers = np.arange(n)
    angles = (numbers[:, None] * numbers[None, :] % n) * (2.0 * math.pi / n)
    table = jnp.asarray(np.cos(angles) + np.sin(angles), jnp.float32)
    high, low = parts_of(table)
    left = jnp.block([[high, high], [low, low]])
    right = jnp.block([[high, low], [high, low]])
    signed = np.where(numbers < n // 2, numbers, numbers - n) * (2.0 * math.pi / n)
    screen = (4.0 * math.pi / n) ** 2
    waves = jnp.asarray(signed[:, None] ** 2 + signed[None, :] ** 2 + screen, jnp.float32)
    volume = 1.0 / n**3
    f32 = jnp.float32
    dma = pltpu.SemaphoreType.DMA
    units = slab // 2
    relay = rounds * units
    scratch = [
        pltpu.VMEM((slab, n, n), f32),
        pltpu.VMEM((slab // 2, n, n), f32),
        pltpu.VMEM((relay, n, n), f32),
        pltpu.VMEM((relay, n, n), f32),
        pltpu.VMEM((rounds, slab, n, n), f32),
        pltpu.VMEM((bands, slab, yb, n), f32),
        pltpu.VMEM((chunks * rounds, n * depth, n), f32),
        pltpu.VMEM((rounds, grids * chunks, (n // grids) * depth, n), f32),
        pltpu.VMEM((chunks * rounds, n * depth, n), f32),
        pltpu.VMEM((slab, n, n), f32),
        pltpu.VMEM((bands, slab, yb, n), f32),
        pltpu.VMEM((bands * bands, 8, n), f32),
        pltpu.VMEM((bands, 8, n), f32),
        pltpu.VMEM((grids, 8, n), f32),
        pltpu.VMEM((n, n), f32),
        dma((2,)),
        dma((units,)),
        dma((units,)),
        dma((relay,)),
        dma((relay,)),
        dma((relay,)),
        dma((relay,)),
        dma((relay,)),
        dma((relay,)),
        dma((bands,)),
        dma((bands,)),
        dma((chunks * rounds * grids,)),
        dma((chunks * rounds * grids,)),
        dma((chunks * rounds * grids,)),
        dma((chunks * rounds * grids,)),
        dma((chunks * bands,)),
        dma((chunks * bands,)),
        dma((bands,)),
        dma((bands,)),
        dma((grids,)),
        dma((grids,)),
    ]
    vmem = pl.BlockSpec(memory_space=pltpu.VMEM)
    return pl.pallas_call(
        functools.partial(whole_kernel, bands, grids, rounds, chunks, 3, 1, n, volume),
        out_shape=jax.ShapeDtypeStruct((bands, slab, yb, n), f32),
        in_specs=[
            pl.BlockSpec(memory_space=pltpu.SMEM),
            pl.BlockSpec(memory_space=pl.ANY),
            vmem, vmem, vmem,
        ],
        out_specs=vmem,
        scratch_shapes=scratch,
        compiler_params=pltpu.CompilerParams(
            collective_id=0, has_side_effects=True, vmem_limit_bytes=60 * 1024 * 1024
        ),
        name="exchange",
    )(sources, orbitals, left, right, waves)


def per_device(orbitals, sources):
    held, slab, full_y, full_z = orbitals.shape
    bands = lax.axis_size("band")
    grids = lax.axis_size("grid")
    n = full_y
    fits = (
        held == 1 and n == full_z == slab * grids and n % 128 == 0 and slab % 16 == 0
        and bands % 2 == 0 and bands * bands <= n and n % (8 * bands) == 0
        and 4 * n * n * slab * (5 * sources.shape[0] + 6) <= 54 * 2**20
    )
    if fits:
        return fused(bands, grids, orbitals, sources)
    return general(orbitals, sources)


def solution(mesh):
    placed = (P("band", "grid", None, None), P())
    return jax.shard_map(
        per_device,
        mesh=mesh,
        in_specs=placed,
        out_specs=P(None, "grid", "band", None),
        check_vma=False,
    )
```

```python
import functools
import math

import jax
import jax.numpy as jnp
import numpy as np
from jax import lax
from jax.experimental import pallas as pl
from jax.experimental.pallas import tpu as pltpu
from jax.sharding import PartitionSpec as P

highest = lax.Precision.HIGHEST
MESH = pl.DeviceIdType.MESH


def spread_2(block, axis, owner):
    block = jnp.where(lax.axis_index(axis) == owner, block, jnp.zeros_like(block))
    return lax.psum(block, axis)


def cas_table(length):
    index_values = jnp.arange(length, dtype=jnp.int32)
    products = index_values[:, None] * index_values[None, :] % length
    angles = products.astype(jnp.float32) * (2.0 * math.pi / length)
    return jnp.cos(angles) + jnp.sin(angles)


def squared_waves(start, count, length):
    index_values = start + jnp.arange(count, dtype=jnp.int32)
    signed = jnp.where(index_values < length // 2, index_values, index_values - length)
    waves = signed.astype(jnp.float32) * (2.0 * math.pi / length)
    return waves * waves


def general(orbitals, sources):
    band_count, slab_x, full_y, full_z = orbitals.shape
    grid_count = lax.axis_size("grid")
    full_x = slab_x * grid_count
    total_bands = band_count * lax.axis_size("band")
    round_count = sources.shape[0]
    table_x = cas_table(full_x)
    table_y = cas_table(full_y)
    table_z = cas_table(full_z)
    column_y = full_y // grid_count
    start_y = lax.axis_index("grid") * column_y
    waves = (
        squared_waves(0, full_x, full_x)[:, None, None]
        + squared_waves(start_y, column_y, full_y)[None, :, None]
        + squared_waves(0, full_z, full_z)[None, None, :]
    )
    screen = (4.0 * math.pi / full_x) ** 2
    volume = 1.0 / (full_x * full_y * full_z)
    kernel = volume / (waves + screen)

    def plane_transform(field):
        spread = jnp.einsum("bxyz,zk->bxyk", field, table_z, precision=highest)
        return jnp.einsum("bxyk,yj->bxjk", spread, table_y, precision=highest)

    def own_slab(number):
        owner = number // band_count
        local = number % band_count
        return (owner, lax.dynamic_index_in_dim(orbitals, local, 0, keepdims=False))

    def fetch(number):
        owner, slab = own_slab(number)
        return spread_2(slab, "band", owner)

    arrived = [fetch(sources[turn]) for turn in range(round_count)]
    terms = jnp.zeros(orbitals.shape, jnp.float32)
    for turn in range(round_count):
        source = arrived[turn][None]
        spectra = plane_transform(orbitals * source)
        potential_columns = lax.all_to_all(spectra, "grid", split_axis=2, concat_axis=1, tiled=True)
        line_spread = jnp.einsum("bxyz,xa->bayz", potential_columns, table_x, precision=highest)
        line_spread = line_spread * kernel[None]
        filtered = jnp.einsum("bayz,ax->bxyz", line_spread, table_x, precision=highest)
        terms = terms + source * plane_transform(
            lax.all_to_all(filtered, "grid", split_axis=1, concat_axis=2, tiled=True)
        )
    orbital_cols, term_cols = (
        lax.all_to_all(orbitals, "band", split_axis=2, concat_axis=0, tiled=True),
        lax.all_to_all(terms, "band", split_axis=2, concat_axis=0, tiled=True),
    )
    flat_orbitals = orbital_cols.reshape(total_bands, -1)
    flat_terms = term_cols.reshape(total_bands, -1)
    partial_intersection = (
        jnp.dot(flat_orbitals, flat_terms.T, precision=highest, preferred_element_type=jnp.float32)
        * volume
    )
    intersection = lax.psum(partial_intersection, ("band", "grid"))
    factor = jnp.linalg.cholesky(intersection)
    solved = lax.linalg.triangular_solve(factor, flat_terms, left_side=True, lower=True)
    return (-solved).reshape(term_cols.shape)


def parts_of(value):
    high = value.astype(jnp.bfloat16)
    low = (value - high.astype(jnp.float32)).astype(jnp.bfloat16)
    return high, low


def along_rows(left, first, second):
    n = first.shape[0]
    h0, l0 = parts_of(first)
    h1, l1 = parts_of(second)
    right = jnp.concatenate(
        [jnp.concatenate([h0, h1], axis=1), jnp.concatenate([l0, l1], axis=1)], axis=0
    )
    both = jnp.dot(left, right, preferred_element_type=jnp.float32)
    return both[:n] + both[n:]


def along_lanes(rows, right):
    n = rows.shape[1]
    high, low = parts_of(rows)
    both = jnp.dot(
        jnp.concatenate([high, low], axis=1), right, preferred_element_type=jnp.float32
    )
    return both[:, :n] + both[:, n:]


def pick(i, values):
    out = values[-1]
    for m in reversed(range(len(values) - 1)):
        out = jnp.where(i == m, values[m], out)
    return out


def whole_kernel(
    bands, grids, rounds, ahead, depth, n, volume,
    sources, orbitals, left_ref, right_ref, waves_ref, out, *scratch,
):
    (own, orb, up, dn, src, fcol, spec, cols, back, terms, pin, tcol, part, sums_b, sums_g, splat,
     in_sem, m_send, m_recv, ox_send, ox_recv, oy_send, oy_recv, or_send, or_recv,
     up_send, up_recv, dn_send, dn_recv, y_send, y_recv, o_send, o_recv, f_send, f_recv,
     b_send, b_recv, p_send, p_recv, t_send, t_recv,
     sb_send, sb_recv, sg_send, sg_recv) = scratch
    b = lax.axis_index("band")
    g = lax.axis_index("grid")
    nz = bands // 2
    z, core = b // 2, b % 2
    slab = n // grids
    half = slab // 2
    yb = n // bands
    pieces = half // depth
    slots = grids * pieces
    quarter = half // 4
    mine = n // 2 * depth
    phases = rounds // 2
    total_units = phases * 2 * half
    lag = (nz - 1) * ahead
    partner = z * 2 + (1 - core)
    gx = g + 1 - 2 * (g % 2)
    gy = lax.rem(g + 2, grids)
    gd = gx + 2 - 4 * (gx // 2)
    column, row = g % 2, g // 2

    barrier = pltpu.get_barrier_semaphore()
    for d in range(1, bands):
        pl.semaphore_signal(barrier, inc=1, device_id=(lax.rem(b + d, bands), g), device_id_type=MESH)
    for d in range(bands):
        pl.semaphore_signal(barrier, inc=1, device_id=(lax.rem(b + d, bands), gy), device_id_type=MESH)
    pl.semaphore_signal(barrier, inc=1, device_id=(b, gx), device_id_type=MESH)
    pl.semaphore_signal(barrier, inc=1, device_id=(b, gd), device_id_type=MESH)
    loads = [
        pltpu.make_async_copy(
            orbitals.at[0, pl.ds((1 - core) * half, half)], own.at[pl.ds((1 - core) * half, half)],
            in_sem.at[0],
        ),
        pltpu.make_async_copy(
            orbitals.at[0, pl.ds(core * half, half)], orb.at[core, g], in_sem.at[1]
        ),
        pltpu.make_async_copy(
            orbitals.at[0, pl.ds(core * half, half)], own.at[pl.ds(core * half, half)], in_sem.at[2]
        ),
    ]
    for load in loads:
        load.start()
    for load in loads:
        load.wait()
    pl.semaphore_wait(barrier, 2 * bands + 1)

    def mate_copy(u, parity):
        return pltpu.make_async_remote_copy(
            src_ref=own.at[pl.ds((1 - core) * half + u * quarter, quarter)],
            dst_ref=orb.at[parity, g, pl.ds(u * quarter, quarter)],
            send_sem=m_send.at[u], recv_sem=m_recv.at[u],
            device_id=(partner, g), device_id_type=MESH,
        )

    def ox_copy(u, which, owner):
        block = orb.at[which, owner, pl.ds(u * quarter, quarter)]
        return pltpu.make_async_remote_copy(
            src_ref=block, dst_ref=block,
            send_sem=ox_send.at[2 * u + which], recv_sem=ox_recv.at[2 * u + which],
            device_id=(b, gx), device_id_type=MESH,
        )

    def oy_copy(u, which, owner):
        block = orb.at[which, owner, pl.ds(u * quarter, quarter)]
        return pltpu.make_async_remote_copy(
            src_ref=block, dst_ref=block,
            send_sem=oy_send.at[u], recv_sem=oy_recv.at[u],
            device_id=(b, gy), device_id_type=MESH,
        )

    def or_copy(u, owner):
        block = orb.at[row, owner, pl.ds(u * quarter, quarter)]
        return pltpu.make_async_remote_copy(
            src_ref=block, dst_ref=block,
            send_sem=or_send.at[u], recv_sem=or_recv.at[u],
            device_id=(b, gx), device_id_type=MESH,
        )

    def up_copy(v):
        return pltpu.make_async_remote_copy(
            src_ref=up.at[v], dst_ref=up.at[v],
            send_sem=up_send.at[v], recv_sem=up_recv.at[v],
            device_id=(lax.rem(b + 2, bands), g), device_id_type=MESH,
        )

    def dn_copy(v):
        return pltpu.make_async_remote_copy(
            src_ref=dn.at[v], dst_ref=dn.at[v],
            send_sem=dn_send.at[v], recv_sem=dn_recv.at[v],
            device_id=(lax.rem(b + bands - 2, bands), g), device_id_type=MESH,
        )

    def place(v):
        q = lax.div(v, 2 * half)
        side = lax.rem(lax.div(v, half), 2)
        return q, side, lax.rem(v, half)

    def y_copy(v, near, far):
        q, side, u = place(v)
        block = src.at[q, jnp.where(side == 0, near, far), u]
        return pltpu.make_async_remote_copy(
            src_ref=block, dst_ref=block,
            send_sem=y_send.at[v], recv_sem=y_recv.at[v],
            device_id=(b, gy), device_id_type=MESH,
        )

    for u in range(4):
        mate_copy(u, core).start()
    for u in range(4):
        mate_copy(u, 1 - core).wait_recv()
        oy_copy(u, 1 - row, g).start()
        for which in range(2):
            ox_copy(u, which, g).start()

    def step(t, _):
        @pl.when(jnp.logical_and(t >= half, jnp.logical_and(t < 2 * half, lax.rem(t, quarter) == 0)))
        def _():
            u = lax.div(t - half, quarter)
            for which in range(2):
                ox_copy(u, which, gx).wait_recv()

        for u in range(4):
            @pl.when(t == quarter * (u + 1) + 3)
            def _():
                oy_copy(u, row, gy).wait_recv()
                or_copy(u, gy).start()

        def pass_on(v, box, copy, first, last):
            @pl.when(jnp.logical_and(v >= 0, v < total_units))
            def _():
                q, side, u = place(v)
                s = sources[phases * column + q]
                at = jnp.where(side == 0, g, gx)
                here = jnp.where(lax.rem(s, 2) == 0, orb[0, at, u], orb[1, at, u])

                @pl.when(first)
                def _():
                    box[v] = here

                @pl.when(jnp.logical_not(first))
                def _():
                    copy(v).wait_recv()
                    box[v] = jnp.where(lax.div(s, 2) == z, here, box[v])

                @pl.when(jnp.logical_not(last))
                def _():
                    copy(v).start()

        pass_on(t - z * ahead, up, up_copy, z == 0, z == nz - 1)
        pass_on(t - (nz - 1 - z) * ahead, dn, dn_copy, z == nz - 1, z == 0)
        v = t - lag

        @pl.when(jnp.logical_and(v >= 0, v < total_units))
        def _():
            q, side, u = place(v)
            s = sources[phases * column + q]
            src[q, jnp.where(side == 0, g, gx), u] = jnp.where(s < 2 * z + 2, up[v], dn[v])
            y_copy(v, g, gx).start()

        return 0

    left = left_ref[...]
    right = right_ref[...]
    base = waves_ref[...]

    def f_copy(q, at, piece, side):
        slot = at * pieces + piece
        return pltpu.make_async_remote_copy(
            src_ref=spec.at[slot, pl.ds((1 - core) * mine, mine)],
            dst_ref=cols.at[q, (at * 2 + side) * pieces + piece],
            send_sem=f_send.at[q * slots + slot], recv_sem=f_recv.at[q * slots + slot],
            device_id=(partner, g), device_id_type=MESH,
        )

    def b_copy(q, at, piece, side):
        slot = at * pieces + piece
        return pltpu.make_async_remote_copy(
            src_ref=cols.at[q, (at * 2 + 1 - side) * pieces + piece],
            dst_ref=back.at[q, slot, pl.ds(side * mine, mine)],
            send_sem=b_send.at[q * slots + slot], recv_sem=b_recv.at[q * slots + slot],
            device_id=(partner, g), device_id_type=MESH,
        )

    order = [(g, 0), (g, 1), (gy, 0), (gx, 0), (gy, 1), (gx, 1), (gd, 0), (gd, 1)]

    def forward(q, i):
        at = pick(i, [a for a, _ in order])
        piece = pick(i, [p for _, p in order])
        far = at == gd

        @pl.when(jnp.logical_or(far, at == gy))
        def _():
            start = q * 2 * half + jnp.where(far, half, 0) + piece * depth

            def arrive(e, _):
                y_copy(start + e, gy, gd).wait_recv()
                return 0

            lax.fori_loop(0, depth, arrive, 0)

        if q == 0:
            @pl.when(far)
            def _():
                for e in range(2):
                    or_copy(2 * piece + e, gd).wait_recv()

        slot = at * pieces + piece
        if q > 0:
            f_copy(q - 1, at, piece, core).wait_send()
        for k in range(0, depth, 2):
            here = pl.ds(piece * depth + k, 2)
            pair = src[q, at, here] * orb[row, at, here]
            rows = along_lanes(pair.reshape(2 * n, n), right)
            planes = along_rows(left, rows[:n], rows[n:])
            spec[slot, pl.ds(k, n, stride=depth), :] = planes[:, :n]
            spec[slot, pl.ds(k + 1, n, stride=depth), :] = planes[:, n:]
        f_copy(q, at, piece, core).start()
        cols[q, (at * 2 + core) * pieces + piece] = spec[slot, pl.ds(core * mine, mine), :]

    def every(q, copy_of):
        for at in range(grids):
            for piece in range(pieces):
                copy_of(q, at, piece)

    lines_count = n // 4

    def lines(q, first, count):
        def line(k, _):
            held = [
                cols[q, :, pl.ds(pl.multiple_of((2 * k + e) * depth, depth), depth), :].reshape(n, n)
                for e in range(2)
            ]
            moved = along_rows(left, held[0], held[1])
            filtered = []
            for e in range(2):
                ky = core * (n // 2) + 2 * k + e
                signed = jnp.where(ky < n // 2, ky, ky - n).astype(jnp.float32)
                wave = signed * (2.0 * math.pi / n)
                filtered.append(moved[:, e * n:(e + 1) * n] * (volume / (base + wave * wave)))
            done = along_rows(left, filtered[0], filtered[1])
            for e in range(2):
                cols[q, :, pl.ds(pl.multiple_of((2 * k + e) * depth, depth), depth), :] = (
                    done[:, e * n:(e + 1) * n].reshape(n // depth, depth, n)
                )
            return 0

        lax.fori_loop(first, first + count, line, 0)

    def inverse(q, at, piece):
        slot = at * pieces + piece
        b_copy(q, at, piece, 1 - core).wait_recv()
        back[q, slot, pl.ds(core * mine, mine), :] = cols[q, (at * 2 + core) * pieces + piece]
        for k in range(0, depth, 2):
            planes = along_rows(
                left,
                back[q, slot, pl.ds(k, n, stride=depth), :],
                back[q, slot, pl.ds(k + 1, n, stride=depth), :],
            )
            rows = jnp.concatenate([planes[:, :n], planes[:, n:]], axis=0)
            potential = along_lanes(rows, right).reshape(2, n, n)
            here = pl.ds(piece * depth + k, 2)
            value = src[q, at, here] * potential
            if q == 0:
                terms[at, here] = value
            else:
                terms[at, here] += value

    def o_copy(target, owner):
        return pltpu.make_async_remote_copy(
            src_ref=own.at[:, pl.ds(target * yb, yb)], dst_ref=fcol.at[owner],
            send_sem=o_send.at[target], recv_sem=o_recv.at[owner],
            device_id=(target, g), device_id_type=MESH,
        )

    def p_copy(at, side, m):
        return pltpu.make_async_remote_copy(
            src_ref=terms.at[at, pl.ds(m * quarter, quarter)],
            dst_ref=pin.at[side, pl.ds(m * quarter, quarter)],
            send_sem=p_send.at[side * 4 + m], recv_sem=p_recv.at[side * 4 + m],
            device_id=(b, gx), device_id_type=MESH,
        )

    def bounds(q, remote):
        local = [q * 2 * half + lag + side * half + (p + 1) * depth for side in range(2) for p in range(2)]
        far = [at + remote for at in local]
        return [local[0], local[1], far[0], local[2], far[1], local[3], far[2], far[3]]

    first_bounds = bounds(0, 10)
    second_bounds = bounds(1, 10)

    def advance(start, stop):
        lax.fori_loop(start, stop, step, 0)

    def first_forward(i, at):
        stop = pick(i, first_bounds)
        advance(at, stop)
        forward(0, i)
        return stop

    at = lax.fori_loop(0, slots, first_forward, 0)
    advance(first_bounds[-1], first_bounds[-1] + 2)
    every(0, lambda q, at, piece: f_copy(q, at, piece, 1 - core).wait_recv())
    settle = first_bounds[-1] + 2

    def first_lines(i, _):
        lines(0, i * (lines_count // slots), lines_count // slots)
        advance(settle + i, settle + i + 1)
        return 0

    lax.fori_loop(0, slots, first_lines, 0)
    every(0, lambda q, at, piece: b_copy(q, at, piece, core).start())
    reached = settle + slots

    def second_forward(i, at):
        stop = jnp.maximum(pick(i, second_bounds), at)
        advance(at, stop)
        inverse(0, lax.div(i, pieces), lax.rem(i, pieces))
        forward(1, i)

        @pl.when(i == 5)
        def _():
            for d in range(1, bands):
                o_copy(lax.rem(b + d, bands), b).start()

        return stop

    lax.fori_loop(0, slots, second_forward, reached)
    every(1, lambda q, at, piece: f_copy(q, at, piece, 1 - core).wait_recv())
    lines(1, 0, lines_count)
    every(1, lambda q, at, piece: b_copy(q, at, piece, core).start())

    fcol[b] = own[:, pl.ds(b * yb, yb), :]
    part[...] = jnp.zeros_like(part)

    def second_inverse(i, _):
        at = pick(lax.div(i, pieces), [gd, gx, gy, g])
        piece = lax.rem(i, pieces)
        inverse(1, at, piece)

        @pl.when(i < 2 * pieces)
        def _():
            for e in range(2):
                p_copy(at, lax.div(i, pieces), 2 * piece + e).start()

        return 0

    lax.fori_loop(0, slots, second_inverse, 0)

    orbital = 2 * z + row

    def t_copy(m, at, target):
        rows = pl.ds(m * quarter, quarter)
        return pltpu.make_async_remote_copy(
            src_ref=terms.at[at, rows, pl.ds(target * yb, yb)],
            dst_ref=tcol.at[orbital, pl.ds(core * half + m * quarter, quarter)],
            send_sem=t_send.at[(jnp.where(at == g, 1, 0) * 4 + m) * bands + target],
            recv_sem=t_recv.at[(orbital * 2 + core) * 4 + m],
            device_id=(target, at), device_id_type=MESH,
        )

    def t_arrival(m, which, side):
        block = tcol.at[which, pl.ds(side * half + m * quarter, quarter)]
        return pltpu.make_async_remote_copy(
            src_ref=block, dst_ref=block,
            send_sem=t_send.at[0], recv_sem=t_recv.at[(which * 2 + side) * 4 + m],
            device_id=(partner, g), device_id_type=MESH,
        )

    def finish(i, _):
        @pl.when(i < 8)
        def _():
            own_side = lax.div(i, 4)
            m = lax.rem(i, 4)
            at = jnp.where(own_side == 0, gy, g)
            rows = pl.ds(m * quarter, quarter)
            p_copy(at, own_side, m).wait_recv()
            terms[at, rows] += pin[own_side, rows]

            @pl.when(own_side == 0)
            def _():
                for target in range(bands):
                    t_copy(m, gy, target).start()

            @pl.when(own_side == 1)
            def _():
                for d in range(1, bands):
                    t_copy(m, g, lax.rem(b + d, bands)).start()
                tcol[orbital, pl.ds(core * half + m * quarter, quarter)] = terms[
                    g, rows, pl.ds(b * yb, yb), :
                ]

        @pl.when(i == 2)
        def _():
            for d in range(1, bands):
                o_copy(b, lax.rem(b + d, bands)).wait_recv()

        @pl.when(i >= 2)
        def _():
            own_side = lax.div(i - 2, 4)
            m = lax.rem(i - 2, 4)
            parity = jnp.where(own_side == 0, 1 - row, row)
            for k in range(nz):
                for side in range(2):
                    local = jnp.logical_and(
                        jnp.logical_and(own_side == 1, z == k), core == side
                    )

                    @pl.when(jnp.logical_not(local))
                    def _():
                        t_arrival(m, 2 * k + parity, side).wait_recv()

            def one(a, _):
                held = [fcol[a, pl.ds(side * half + m * quarter, quarter)] for side in range(2)]
                for k in range(nz):
                    which = 2 * k + parity
                    total = jnp.zeros((8, n), jnp.float32)
                    for side in range(2):
                        prod = held[side] * tcol[which, pl.ds(side * half + m * quarter, quarter)]
                        total = total + jnp.sum(prod.reshape(-1, 8, n), axis=0)
                    part[a * bands + which] += total
                return 0

            lax.fori_loop(0, bands, one, 0)

        return 0

    lax.fori_loop(0, 10, finish, 0)

    count = bands * bands
    flat = jnp.sum(part[...], axis=1)
    if count < n:
        flat = jnp.concatenate([flat, jnp.zeros((n - count, n), jnp.float32)], axis=0)
    lanes = jnp.sum(flat.T, axis=0, keepdims=True)
    sums_b[b] = jnp.broadcast_to(lanes, (8, n))

    def sb_copy(target, owner):
        return pltpu.make_async_remote_copy(
            src_ref=sums_b.at[b], dst_ref=sums_b.at[owner],
            send_sem=sb_send.at[target], recv_sem=sb_recv.at[owner],
            device_id=(target, g), device_id_type=MESH,
        )

    def sg_copy(target, owner):
        return pltpu.make_async_remote_copy(
            src_ref=sums_g.at[g], dst_ref=sums_g.at[owner],
            send_sem=sg_send.at[target], recv_sem=sg_recv.at[owner],
            device_id=(b, target), device_id_type=MESH,
        )

    for d in range(1, bands):
        sb_copy(lax.rem(b + d, bands), b).start()
    for d in range(1, bands):
        sb_copy(b, lax.rem(b + d, bands)).wait_recv()
    sums_g[g] = jnp.sum(sums_b[...], axis=0)
    for d in range(1, grids):
        sg_copy(lax.rem(g + d, grids), g).start()
    for d in range(1, grids):
        sg_copy(g, lax.rem(g + d, grids)).wait_recv()
    total = jnp.sum(sums_g[...], axis=0)[:1] * volume
    splat[...] = jnp.broadcast_to(total, (n, n)).T

    def entry(i, k):
        first = splat[pl.ds(i * bands + k, 1), :]
        return 0.5 * (first + splat[pl.ds(k * bands + i, 1), :])

    factor = {}
    inverse_diag = {}
    for k in range(bands):
        diag = entry(k, k)
        for m in range(k):
            diag = diag - factor[k, m] * factor[k, m]
        inverse_diag[k] = 1.0 / jnp.sqrt(diag)
        for i in range(k + 1, bands):
            value = entry(i, k)
            for m in range(k):
                value = value - factor[i, m] * factor[k, m]
            factor[i, k] = value * inverse_diag[k]
    for k in range(bands):
        splat[pl.ds(k * bands + k, 1), :] = inverse_diag[k]
        for i in range(k + 1, bands):
            splat[pl.ds(i * bands + k, 1), :] = factor[i, k]

    def solve(p, _):
        x = pl.ds(4 * p, 4)
        solved = []
        for i in range(bands):
            value = -tcol[i, x]
            for k in range(i):
                value = value - splat[pl.ds(i * bands + k, 1), :] * solved[k]
            value = value * splat[pl.ds(i * bands + i, 1), :]
            out[i, x] = value
            solved.append(value)
        return 0

    lax.fori_loop(0, slab // 4, solve, 0)

    for u in range(4):
        mate_copy(u, core).wait_send()
        oy_copy(u, 1 - row, g).wait_send()
        or_copy(u, gy).wait_send()
        for which in range(2):
            ox_copy(u, which, g).wait_send()

    def settle_units(v, _):
        @pl.when(z < nz - 1)
        def _():
            up_copy(v).wait_send()

        @pl.when(z > 0)
        def _():
            dn_copy(v).wait_send()

        y_copy(v, g, gx).wait_send()
        return 0

    lax.fori_loop(0, total_units, settle_units, 0)
    every(phases - 1, lambda q, at, piece: f_copy(q, at, piece, core).wait_send())
    for q in range(phases):
        every(q, lambda q, at, piece: b_copy(q, at, piece, core).wait_send())
    for m in range(4):
        p_copy(gd, 0, m).wait_send()
        p_copy(gx, 1, m).wait_send()
        for target in range(bands):
            t_copy(m, gy, target).wait_send()
        for d in range(1, bands):
            t_copy(m, g, lax.rem(b + d, bands)).wait_send()
    for d in range(1, bands):
        o_copy(lax.rem(b + d, bands), b).wait_send()
        sb_copy(lax.rem(b + d, bands), b).wait_send()
    for d in range(1, grids):
        sg_copy(lax.rem(g + d, grids), g).wait_send()


def fused(bands, grids, orbitals, sources):
    n = orbitals.shape[2]
    rounds = sources.shape[0]
    slab = n // grids
    half = slab // 2
    depth = 8
    pieces = half // depth
    slots = grids * pieces
    phases = rounds // 2
    yb = n // bands
    numbers = np.arange(n)
    angles = (numbers[:, None] * numbers[None, :] % n) * (2.0 * math.pi / n)
    table = jnp.asarray(np.cos(angles) + np.sin(angles), jnp.float32)
    high, low = parts_of(table)
    left = jnp.block([[high, high], [low, low]])
    right = jnp.block([[high, low], [high, low]])
    signed = np.where(numbers < n // 2, numbers, numbers - n) * (2.0 * math.pi / n)
    screen = (4.0 * math.pi / n) ** 2
    waves = jnp.asarray(signed[:, None] ** 2 + signed[None, :] ** 2 + screen, jnp.float32)
    volume = 1.0 / n**3
    f32 = jnp.float32
    dma = pltpu.SemaphoreType.DMA
    relay = phases * 2 * half
    scratch = [
        pltpu.VMEM((slab, n, n), f32),
        pltpu.VMEM((2, grids, half, n, n), f32),
        pltpu.VMEM((relay, n, n), f32),
        pltpu.VMEM((relay, n, n), f32),
        pltpu.VMEM((phases, grids, half, n, n), f32),
        pltpu.VMEM((bands, slab, yb, n), f32),
        pltpu.VMEM((slots, n * depth, n), f32),
        pltpu.VMEM((phases, n // depth, n // 2 * depth, n), f32),
        pltpu.VMEM((phases, slots, n * depth, n), f32),
        pltpu.VMEM((grids, half, n, n), f32),
        pltpu.VMEM((2, half, n, n), f32),
        pltpu.VMEM((bands, slab, yb, n), f32),
        pltpu.VMEM((bands * bands, 8, n), f32),
        pltpu.VMEM((bands, 8, n), f32),
        pltpu.VMEM((grids, 8, n), f32),
        pltpu.VMEM((n, n), f32),
        dma((3,)),
        dma((4,)), dma((4,)),
        dma((8,)), dma((8,)),
        dma((4,)), dma((4,)),
        dma((4,)), dma((4,)),
        dma((relay,)), dma((relay,)),
        dma((relay,)), dma((relay,)),
        dma((relay,)), dma((relay,)),
        dma((bands,)), dma((bands,)),
        dma((phases * slots,)), dma((phases * slots,)),
        dma((phases * slots,)), dma((phases * slots,)),
        dma((8,)), dma((8,)),
        dma((8 * bands,)), dma((8 * bands,)),
        dma((bands,)), dma((bands,)),
        dma((grids,)), dma((grids,)),
    ]
    vmem = pl.BlockSpec(memory_space=pltpu.VMEM)
    return pl.pallas_call(
        functools.partial(whole_kernel, bands, grids, rounds, 3, depth, n, volume),
        out_shape=jax.ShapeDtypeStruct((bands, slab, yb, n), f32),
        in_specs=[
            pl.BlockSpec(memory_space=pltpu.SMEM),
            pl.BlockSpec(memory_space=pl.ANY),
            vmem, vmem, vmem,
        ],
        out_specs=vmem,
        scratch_shapes=scratch,
        compiler_params=pltpu.CompilerParams(
            collective_id=0, has_side_effects=True, vmem_limit_bytes=63 * 1024 * 1024
        ),
        name="exchange",
    )(sources, orbitals, left, right, waves)


def per_device(orbitals, sources):
    held, slab, full_y, full_z = orbitals.shape
    bands = lax.axis_size("band")
    grids = lax.axis_size("grid")
    n = full_y
    rounds = sources.shape[0]
    fits = (
        held == 1 and n == full_z == slab * grids and n % 128 == 0 and slab % 32 == 0
        and grids == 4 and rounds == grids and bands % 2 == 0 and bands * bands <= n
        and n % (8 * bands) == 0 and 4 * n * n * slab * 29 <= 60 * 2**20
    )
    if fits:
        return fused(bands, grids, orbitals, sources)
    return general(orbitals, sources)


def solution(mesh):
    placed = (P("band", "grid", None, None), P())
    return jax.shard_map(
        per_device,
        mesh=mesh,
        in_specs=placed,
        out_specs=P(None, "grid", "band", None),
        check_vma=False,
    )
```

```python
import functools
import math

import jax
import jax.numpy as jnp
import numpy as np
from jax import lax
from jax.experimental import pallas as pl
from jax.experimental.pallas import tpu as pltpu
from jax.sharding import PartitionSpec as P

highest = lax.Precision.HIGHEST
MESH = pl.DeviceIdType.MESH


def spread_2(block, axis, owner):
    block = jnp.where(lax.axis_index(axis) == owner, block, jnp.zeros_like(block))
    return lax.psum(block, axis)


def cas_table(length):
    index_values = jnp.arange(length, dtype=jnp.int32)
    products = index_values[:, None] * index_values[None, :] % length
    angles = products.astype(jnp.float32) * (2.0 * math.pi / length)
    return jnp.cos(angles) + jnp.sin(angles)


def squared_waves(start, count, length):
    index_values = start + jnp.arange(count, dtype=jnp.int32)
    signed = jnp.where(index_values < length // 2, index_values, index_values - length)
    waves = signed.astype(jnp.float32) * (2.0 * math.pi / length)
    return waves * waves


def general(orbitals, sources):
    band_count, slab_x, full_y, full_z = orbitals.shape
    grid_count = lax.axis_size("grid")
    full_x = slab_x * grid_count
    total_bands = band_count * lax.axis_size("band")
    round_count = sources.shape[0]
    table_x = cas_table(full_x)
    table_y = cas_table(full_y)
    table_z = cas_table(full_z)
    column_y = full_y // grid_count
    start_y = lax.axis_index("grid") * column_y
    waves = (
        squared_waves(0, full_x, full_x)[:, None, None]
        + squared_waves(start_y, column_y, full_y)[None, :, None]
        + squared_waves(0, full_z, full_z)[None, None, :]
    )
    screen = (4.0 * math.pi / full_x) ** 2
    volume = 1.0 / (full_x * full_y * full_z)
    kernel = volume / (waves + screen)

    def plane_transform(field):
        spread = jnp.einsum("bxyz,zk->bxyk", field, table_z, precision=highest)
        return jnp.einsum("bxyk,yj->bxjk", spread, table_y, precision=highest)

    def own_slab(number):
        owner = number // band_count
        local = number % band_count
        return (owner, lax.dynamic_index_in_dim(orbitals, local, 0, keepdims=False))

    def fetch(number):
        owner, slab = own_slab(number)
        return spread_2(slab, "band", owner)

    arrived = [fetch(sources[turn]) for turn in range(round_count)]
    terms = jnp.zeros(orbitals.shape, jnp.float32)
    for turn in range(round_count):
        source = arrived[turn][None]
        spectra = plane_transform(orbitals * source)
        potential_columns = lax.all_to_all(spectra, "grid", split_axis=2, concat_axis=1, tiled=True)
        line_spread = jnp.einsum("bxyz,xa->bayz", potential_columns, table_x, precision=highest)
        line_spread = line_spread * kernel[None]
        filtered = jnp.einsum("bayz,ax->bxyz", line_spread, table_x, precision=highest)
        terms = terms + source * plane_transform(
            lax.all_to_all(filtered, "grid", split_axis=1, concat_axis=2, tiled=True)
        )
    orbital_cols, term_cols = (
        lax.all_to_all(orbitals, "band", split_axis=2, concat_axis=0, tiled=True),
        lax.all_to_all(terms, "band", split_axis=2, concat_axis=0, tiled=True),
    )
    flat_orbitals = orbital_cols.reshape(total_bands, -1)
    flat_terms = term_cols.reshape(total_bands, -1)
    partial_intersection = (
        jnp.dot(flat_orbitals, flat_terms.T, precision=highest, preferred_element_type=jnp.float32)
        * volume
    )
    intersection = lax.psum(partial_intersection, ("band", "grid"))
    factor = jnp.linalg.cholesky(intersection)
    solved = lax.linalg.triangular_solve(factor, flat_terms, left_side=True, lower=True)
    return (-solved).reshape(term_cols.shape)


def parts_of(value):
    high = value.astype(jnp.bfloat16)
    low = (value - high.astype(jnp.float32)).astype(jnp.bfloat16)
    return high, low


def along_rows(left, first, second):
    n = first.shape[0]
    h0, l0 = parts_of(first)
    h1, l1 = parts_of(second)
    right = jnp.concatenate(
        [jnp.concatenate([h0, h1], axis=1), jnp.concatenate([l0, l1], axis=1)], axis=0
    )
    both = jnp.dot(left, right, preferred_element_type=jnp.float32)
    return both[:n] + both[n:]


def along_lanes(rows, right):
    n = rows.shape[1]
    high, low = parts_of(rows)
    both = jnp.dot(
        jnp.concatenate([high, low], axis=1), right, preferred_element_type=jnp.float32
    )
    return both[:, :n] + both[:, n:]


def pick(i, values):
    out = values[-1]
    for m in reversed(range(len(values) - 1)):
        out = jnp.where(i == m, values[m], out)
    return out


def whole_kernel(
    bands, grids, rounds, ahead, early, depth, n, volume,
    sources, orbitals, left_ref, right_ref, waves_ref, out, *scratch,
):
    (own, orb, up, dn, src, fcol, spec, cols, back, terms, pin, tcol, part, sums_b, sums_g, splat,
     in_sem, m_send, m_recv, ox_send, ox_recv, oy_send, oy_recv, or_send, or_recv,
     up_send, up_recv, dn_send, dn_recv, y_send, y_recv, o_send, o_recv, f_send, f_recv,
     b_send, b_recv, p_send, p_recv, t_send, t_recv,
     sb_send, sb_recv, sg_send, sg_recv) = scratch
    b = lax.axis_index("band")
    g = lax.axis_index("grid")
    nz = bands // 2
    z, core = b // 2, b % 2
    slab = n // grids
    half = slab // 2
    yb = n // bands
    pieces = half // depth
    slots = grids * pieces
    quarter = half // 4
    pair = 2
    pairs = half // pair
    mine = n // 2 * depth
    phases = rounds // 2
    total_units = phases * 2 * half
    lag = (nz - 1) * ahead
    partner = z * 2 + (1 - core)
    gx = g + 1 - 2 * (g % 2)
    gy = lax.rem(g + 2, grids)
    gd = gx + 2 - 4 * (gx // 2)
    column, row = g % 2, g // 2

    barrier = pltpu.get_barrier_semaphore()
    for d in range(1, bands):
        pl.semaphore_signal(barrier, inc=1, device_id=(lax.rem(b + d, bands), g), device_id_type=MESH)
    for d in range(bands):
        pl.semaphore_signal(barrier, inc=1, device_id=(lax.rem(b + d, bands), gy), device_id_type=MESH)
    pl.semaphore_signal(barrier, inc=1, device_id=(b, gx), device_id_type=MESH)
    pl.semaphore_signal(barrier, inc=1, device_id=(b, gd), device_id_type=MESH)
    loads = [
        pltpu.make_async_copy(
            orbitals.at[0, pl.ds((1 - core) * half, half)], own.at[pl.ds((1 - core) * half, half)],
            in_sem.at[0],
        ),
        pltpu.make_async_copy(
            orbitals.at[0, pl.ds(core * half, half)], orb.at[core, g], in_sem.at[1]
        ),
        pltpu.make_async_copy(
            orbitals.at[0, pl.ds(core * half, half)], own.at[pl.ds(core * half, half)], in_sem.at[2]
        ),
    ]
    for load in loads:
        load.start()
    for load in loads:
        load.wait()
    pl.semaphore_wait(barrier, 2 * bands + 1)

    def mate_copy(u, parity):
        return pltpu.make_async_remote_copy(
            src_ref=own.at[pl.ds((1 - core) * half + u * quarter, quarter)],
            dst_ref=orb.at[parity, g, pl.ds(u * quarter, quarter)],
            send_sem=m_send.at[u], recv_sem=m_recv.at[u],
            device_id=(partner, g), device_id_type=MESH,
        )

    def ox_copy(u, which, owner):
        block = orb.at[which, owner, pl.ds(u * quarter, quarter)]
        return pltpu.make_async_remote_copy(
            src_ref=block, dst_ref=block,
            send_sem=ox_send.at[2 * u + which], recv_sem=ox_recv.at[2 * u + which],
            device_id=(b, gx), device_id_type=MESH,
        )

    def oy_copy(u, which, owner):
        block = orb.at[which, owner, pl.ds(u * quarter, quarter)]
        return pltpu.make_async_remote_copy(
            src_ref=block, dst_ref=block,
            send_sem=oy_send.at[u], recv_sem=oy_recv.at[u],
            device_id=(b, gy), device_id_type=MESH,
        )

    def or_copy(u, owner):
        block = orb.at[row, owner, pl.ds(u * quarter, quarter)]
        return pltpu.make_async_remote_copy(
            src_ref=block, dst_ref=block,
            send_sem=or_send.at[u], recv_sem=or_recv.at[u],
            device_id=(b, gx), device_id_type=MESH,
        )

    def up_copy(v):
        return pltpu.make_async_remote_copy(
            src_ref=up.at[v], dst_ref=up.at[v],
            send_sem=up_send.at[v], recv_sem=up_recv.at[v],
            device_id=(lax.rem(b + 2, bands), g), device_id_type=MESH,
        )

    def dn_copy(v):
        return pltpu.make_async_remote_copy(
            src_ref=dn.at[v], dst_ref=dn.at[v],
            send_sem=dn_send.at[v], recv_sem=dn_recv.at[v],
            device_id=(lax.rem(b + bands - 2, bands), g), device_id_type=MESH,
        )

    def place(v):
        q = lax.div(v, 2 * half)
        side = lax.rem(lax.div(v, half), 2)
        return q, side, lax.rem(v, half)

    def y_copy(v, near, far):
        q, side, u = place(v)
        block = src.at[q, jnp.where(side == 0, near, far), u]
        return pltpu.make_async_remote_copy(
            src_ref=block, dst_ref=block,
            send_sem=y_send.at[v], recv_sem=y_recv.at[v],
            device_id=(b, gy), device_id_type=MESH,
        )

    def o_copy(target, owner, late):
        planes = pl.ds(early, slab - early) if late else pl.ds(0, early)
        return pltpu.make_async_remote_copy(
            src_ref=own.at[planes, pl.ds(target * yb, yb)], dst_ref=fcol.at[owner, planes],
            send_sem=o_send.at[late * bands + target], recv_sem=o_recv.at[late * bands + owner],
            device_id=(target, g), device_id_type=MESH,
        )

    for u in range(4):
        mate_copy(u, core).start()
    for d in range(1, bands):
        o_copy(lax.rem(b + d, bands), b, 0).start()
    for u in range(4):
        mate_copy(u, 1 - core).wait_recv()
        oy_copy(u, 1 - row, g).start()
        for which in range(2):
            ox_copy(u, which, g).start()

    def step(t, _):
        @pl.when(jnp.logical_and(t >= half, jnp.logical_and(t < 2 * half, lax.rem(t, quarter) == 0)))
        def _():
            u = lax.div(t - half, quarter)
            for which in range(2):
                ox_copy(u, which, gx).wait_recv()

        for u in range(4):
            @pl.when(t == quarter * (u + 1) + 3)
            def _():
                oy_copy(u, row, gy).wait_recv()
                or_copy(u, gy).start()

        def pass_on(v, box, copy, first, last):
            @pl.when(jnp.logical_and(v >= 0, v < total_units))
            def _():
                q, side, u = place(v)
                s = sources[phases * column + q]
                at = jnp.where(side == 0, g, gx)
                here = jnp.where(lax.rem(s, 2) == 0, orb[0, at, u], orb[1, at, u])

                @pl.when(first)
                def _():
                    box[v] = here

                @pl.when(jnp.logical_not(first))
                def _():
                    copy(v).wait_recv()
                    box[v] = jnp.where(lax.div(s, 2) == z, here, box[v])

                @pl.when(jnp.logical_not(last))
                def _():
                    copy(v).start()

        pass_on(t - z * ahead, up, up_copy, z == 0, z == nz - 1)
        pass_on(t - (nz - 1 - z) * ahead, dn, dn_copy, z == nz - 1, z == 0)
        v = t - lag

        @pl.when(jnp.logical_and(v >= 0, v < total_units))
        def _():
            q, side, u = place(v)
            s = sources[phases * column + q]
            src[q, jnp.where(side == 0, g, gx), u] = jnp.where(s < 2 * z + 2, up[v], dn[v])
            y_copy(v, g, gx).start()

        return 0

    left = left_ref[...]
    right = right_ref[...]
    base = waves_ref[...]

    def f_copy(q, at, piece, side):
        slot = at * pieces + piece
        return pltpu.make_async_remote_copy(
            src_ref=spec.at[slot, pl.ds((1 - core) * mine, mine)],
            dst_ref=cols.at[q, (at * 2 + side) * pieces + piece],
            send_sem=f_send.at[q * slots + slot], recv_sem=f_recv.at[q * slots + slot],
            device_id=(partner, g), device_id_type=MESH,
        )

    def b_copy(q, at, piece, side):
        slot = at * pieces + piece
        return pltpu.make_async_remote_copy(
            src_ref=cols.at[q, (at * 2 + 1 - side) * pieces + piece],
            dst_ref=back.at[q, slot, pl.ds(side * mine, mine)],
            send_sem=b_send.at[q * slots + slot], recv_sem=b_recv.at[q * slots + slot],
            device_id=(partner, g), device_id_type=MESH,
        )

    order = [(g, 0), (g, 1), (gy, 0), (gx, 0), (gy, 1), (gx, 1), (gd, 0), (gd, 1)]

    def forward(q, i):
        at = pick(i, [a for a, _ in order])
        piece = pick(i, [p for _, p in order])
        far = at == gd

        @pl.when(jnp.logical_or(far, at == gy))
        def _():
            start = q * 2 * half + jnp.where(far, half, 0) + piece * depth

            def arrive(e, _):
                y_copy(start + e, gy, gd).wait_recv()
                return 0

            lax.fori_loop(0, depth, arrive, 0)

        if q == 0:
            @pl.when(far)
            def _():
                for e in range(2):
                    or_copy(2 * piece + e, gd).wait_recv()

        slot = at * pieces + piece
        if q > 0:
            f_copy(q - 1, at, piece, core).wait_send()
        for k in range(0, depth, 2):
            here = pl.ds(piece * depth + k, 2)
            pair = src[q, at, here] * orb[row, at, here]
            rows = along_lanes(pair.reshape(2 * n, n), right)
            planes = along_rows(left, rows[:n], rows[n:])
            spec[slot, pl.ds(k, n, stride=depth), :] = planes[:, :n]
            spec[slot, pl.ds(k + 1, n, stride=depth), :] = planes[:, n:]
        f_copy(q, at, piece, core).start()
        cols[q, (at * 2 + core) * pieces + piece] = spec[slot, pl.ds(core * mine, mine), :]

    def every(q, copy_of):
        for at in range(grids):
            for piece in range(pieces):
                copy_of(q, at, piece)

    lines_count = n // 4

    def lines(q, first, count):
        def line(k):
            held = [
                cols[q, :, pl.ds(pl.multiple_of((2 * k + e) * depth, depth), depth), :].reshape(n, n)
                for e in range(2)
            ]
            moved = along_rows(left, held[0], held[1])
            filtered = []
            for e in range(2):
                ky = core * (n // 2) + 2 * k + e
                signed = jnp.where(ky < n // 2, ky, ky - n).astype(jnp.float32)
                wave = signed * (2.0 * math.pi / n)
                filtered.append(moved[:, e * n:(e + 1) * n] * (volume / (base + wave * wave)))
            done = along_rows(left, filtered[0], filtered[1])
            for e in range(2):
                cols[q, :, pl.ds(pl.multiple_of((2 * k + e) * depth, depth), depth), :] = (
                    done[:, e * n:(e + 1) * n].reshape(n // depth, depth, n)
                )

        def group(i, _):
            for e in range(2):
                line(first + 2 * i + e)
            return 0

        lax.fori_loop(0, count // 2, group, 0)

    def inverse(q, at, piece):
        slot = at * pieces + piece
        b_copy(q, at, piece, 1 - core).wait_recv()
        back[q, slot, pl.ds(core * mine, mine), :] = cols[q, (at * 2 + core) * pieces + piece]
        for k in range(0, depth, 2):
            planes = along_rows(
                left,
                back[q, slot, pl.ds(k, n, stride=depth), :],
                back[q, slot, pl.ds(k + 1, n, stride=depth), :],
            )
            rows = jnp.concatenate([planes[:, :n], planes[:, n:]], axis=0)
            potential = along_lanes(rows, right).reshape(2, n, n)
            here = pl.ds(piece * depth + k, 2)
            value = src[q, at, here] * potential
            if q == 0:
                terms[at, here] = value
            else:
                terms[at, here] += value

    def p_copy(at, side, m):
        return pltpu.make_async_remote_copy(
            src_ref=terms.at[at, pl.ds(m * pair, pair)],
            dst_ref=pin.at[side, pl.ds(m * pair, pair)],
            send_sem=p_send.at[side * pairs + m], recv_sem=p_recv.at[side * pairs + m],
            device_id=(b, gx), device_id_type=MESH,
        )

    def bounds(q, remote):
        local = [q * 2 * half + lag + side * half + (p + 1) * depth for side in range(2) for p in range(2)]
        far = [at + remote for at in local]
        last = [far[2] + 6, far[3] + 1] if q == 0 else far[2:]
        return [local[0], local[1], far[0], local[2], far[1], local[3], *last]

    first_bounds = bounds(0, 10)
    second_bounds = bounds(1, 10)

    def advance(start, stop):
        lax.fori_loop(start, stop, step, 0)

    def first_forward(i, at):
        stop = pick(i, first_bounds)
        advance(at, stop)
        forward(0, i)
        return stop

    at = lax.fori_loop(0, slots, first_forward, 0)
    advance(first_bounds[-1], first_bounds[-1] + 2)
    every(0, lambda q, at, piece: f_copy(q, at, piece, 1 - core).wait_recv())
    settle = first_bounds[-1] + 2

    def first_lines(i, _):
        lines(0, i * (lines_count // slots), lines_count // slots)
        advance(settle + i, settle + i + 1)
        return 0

    lax.fori_loop(0, slots, first_lines, 0)
    every(0, lambda q, at, piece: b_copy(q, at, piece, core).start())
    reached = settle + slots

    def second_forward(i, at):
        stop = jnp.maximum(pick(i, second_bounds), at)
        advance(at, stop)
        inverse(0, lax.div(i, pieces), lax.rem(i, pieces))
        forward(1, i)

        @pl.when(i == 5)
        def _():
            for d in range(1, bands):
                o_copy(lax.rem(b + d, bands), b, 1).start()

        return stop

    lax.fori_loop(0, slots, second_forward, reached)
    every(1, lambda q, at, piece: f_copy(q, at, piece, 1 - core).wait_recv())
    lines(1, 0, lines_count)
    every(1, lambda q, at, piece: b_copy(q, at, piece, core).start())

    fcol[b] = own[:, pl.ds(b * yb, yb), :]
    part[...] = jnp.zeros_like(part)

    def second_inverse(i, _):
        at = pick(lax.div(i, pieces), [gd, gx, gy, g])
        piece = lax.rem(i, pieces)
        inverse(1, at, piece)

        @pl.when(i < 2 * pieces)
        def _():
            for e in range(depth // pair):
                p_copy(at, lax.div(i, pieces), depth // pair * piece + e).start()

        return 0

    lax.fori_loop(0, slots, second_inverse, 0)

    orbital = 2 * z + row

    wait = 3
    def t_copy(m, at, target):
        rows = pl.ds(m * pair, pair)
        return pltpu.make_async_remote_copy(
            src_ref=terms.at[at, rows, pl.ds(target * yb, yb)],
            dst_ref=tcol.at[orbital, pl.ds(core * half + m * pair, pair)],
            send_sem=t_send.at[(jnp.where(at == g, 1, 0) * pairs + m) * bands + target],
            recv_sem=t_recv.at[(orbital * 2 + core) * pairs + m],
            device_id=(target, at), device_id_type=MESH,
        )

    def t_arrival(m, which, side):
        block = tcol.at[which, pl.ds(side * half + m * pair, pair)]
        return pltpu.make_async_remote_copy(
            src_ref=block, dst_ref=block,
            send_sem=t_send.at[0], recv_sem=t_recv.at[(which * 2 + side) * pairs + m],
            device_id=(partner, g), device_id_type=MESH,
        )

    def finish(i, _):
        @pl.when(i < 2 * pairs)
        def _():
            own_side = lax.div(i, pairs)
            m = lax.rem(i, pairs)
            at = jnp.where(own_side == 0, gy, g)
            rows = pl.ds(m * pair, pair)
            p_copy(at, own_side, m).wait_recv()
            terms[at, rows] += pin[own_side, rows]

            @pl.when(own_side == 0)
            def _():
                for target in range(bands):
                    t_copy(m, gy, target).start()

            @pl.when(own_side == 1)
            def _():
                for d in range(1, bands):
                    t_copy(m, g, lax.rem(b + d, bands)).start()
                tcol[orbital, pl.ds(core * half + m * pair, pair)] = terms[
                    g, rows, pl.ds(b * yb, yb), :
                ]

        @pl.when(i == wait)
        def _():
            for d in range(1, bands):
                for late in range(2):
                    o_copy(b, lax.rem(b + d, bands), late).wait_recv()

        @pl.when(i >= wait)
        def _():
            own_side = lax.div(i - wait, pairs)
            m = lax.rem(i - wait, pairs)
            parity = jnp.where(own_side == 0, 1 - row, row)
            for k in range(nz):
                for side in range(2):
                    local = jnp.logical_and(
                        jnp.logical_and(own_side == 1, z == k), core == side
                    )

                    @pl.when(jnp.logical_not(local))
                    def _():
                        t_arrival(m, 2 * k + parity, side).wait_recv()

            def one(a, _):
                held = [fcol[a, pl.ds(side * half + m * pair, pair)] for side in range(2)]
                for k in range(nz):
                    which = 2 * k + parity
                    total = jnp.zeros((8, n), jnp.float32)
                    for side in range(2):
                        prod = held[side] * tcol[which, pl.ds(side * half + m * pair, pair)]
                        total = total + jnp.sum(prod.reshape(-1, 8, n), axis=0)
                    part[a * bands + which] += total
                return 0

            lax.fori_loop(0, bands, one, 0)

        return 0

    lax.fori_loop(0, 2 * pairs + wait, finish, 0)

    count = bands * bands
    flat = jnp.sum(part[...], axis=1)
    if count < n:
        flat = jnp.concatenate([flat, jnp.zeros((n - count, n), jnp.float32)], axis=0)
    lanes = jnp.sum(flat.T, axis=0, keepdims=True)
    sums_b[b] = jnp.broadcast_to(lanes, (8, n))

    def sb_copy(target, owner):
        return pltpu.make_async_remote_copy(
            src_ref=sums_b.at[b], dst_ref=sums_b.at[owner],
            send_sem=sb_send.at[target], recv_sem=sb_recv.at[owner],
            device_id=(target, g), device_id_type=MESH,
        )

    def sg_copy(target, owner):
        return pltpu.make_async_remote_copy(
            src_ref=sums_g.at[g], dst_ref=sums_g.at[owner],
            send_sem=sg_send.at[target], recv_sem=sg_recv.at[owner],
            device_id=(b, target), device_id_type=MESH,
        )

    for d in range(1, bands):
        sb_copy(lax.rem(b + d, bands), b).start()
    for d in range(1, bands):
        sb_copy(b, lax.rem(b + d, bands)).wait_recv()
    sums_g[g] = jnp.sum(sums_b[...], axis=0)
    for d in range(1, grids):
        sg_copy(lax.rem(g + d, grids), g).start()
    for d in range(1, grids):
        sg_copy(g, lax.rem(g + d, grids)).wait_recv()
    total = jnp.sum(sums_g[...], axis=0)[:1] * volume
    splat[...] = jnp.broadcast_to(total, (n, n)).T

    def entry(i, k):
        first = splat[pl.ds(i * bands + k, 1), :]
        return 0.5 * (first + splat[pl.ds(k * bands + i, 1), :])

    factor = {}
    inverse_diag = {}
    for k in range(bands):
        diag = entry(k, k)
        for m in range(k):
            diag = diag - factor[k, m] * factor[k, m]
        inverse_diag[k] = 1.0 / jnp.sqrt(diag)
        for i in range(k + 1, bands):
            value = entry(i, k)
            for m in range(k):
                value = value - factor[i, m] * factor[k, m]
            factor[i, k] = value * inverse_diag[k]
    for k in range(bands):
        splat[pl.ds(k * bands + k, 1), :] = inverse_diag[k]
        for i in range(k + 1, bands):
            splat[pl.ds(i * bands + k, 1), :] = factor[i, k]

    def solve(p, _):
        x = pl.ds(4 * p, 4)
        solved = []
        for i in range(bands):
            value = -tcol[i, x]
            for k in range(i):
                value = value - splat[pl.ds(i * bands + k, 1), :] * solved[k]
            value = value * splat[pl.ds(i * bands + i, 1), :]
            out[i, x] = value
            solved.append(value)
        return 0

    lax.fori_loop(0, slab // 4, solve, 0)

    for u in range(4):
        mate_copy(u, core).wait_send()
        oy_copy(u, 1 - row, g).wait_send()
        or_copy(u, gy).wait_send()
        for which in range(2):
            ox_copy(u, which, g).wait_send()

    def settle_units(v, _):
        @pl.when(z < nz - 1)
        def _():
            up_copy(v).wait_send()

        @pl.when(z > 0)
        def _():
            dn_copy(v).wait_send()

        y_copy(v, g, gx).wait_send()
        return 0

    lax.fori_loop(0, total_units, settle_units, 0)
    every(phases - 1, lambda q, at, piece: f_copy(q, at, piece, core).wait_send())
    for q in range(phases):
        every(q, lambda q, at, piece: b_copy(q, at, piece, core).wait_send())
    for m in range(pairs):
        p_copy(gd, 0, m).wait_send()
        p_copy(gx, 1, m).wait_send()
        for target in range(bands):
            t_copy(m, gy, target).wait_send()
        for d in range(1, bands):
            t_copy(m, g, lax.rem(b + d, bands)).wait_send()
    for d in range(1, bands):
        for late in range(2):
            o_copy(lax.rem(b + d, bands), b, late).wait_send()
        sb_copy(lax.rem(b + d, bands), b).wait_send()
    for d in range(1, grids):
        sg_copy(lax.rem(g + d, grids), g).wait_send()


def fused(bands, grids, orbitals, sources):
    n = orbitals.shape[2]
    rounds = sources.shape[0]
    slab = n // grids
    half = slab // 2
    depth = 8
    pieces = half // depth
    slots = grids * pieces
    phases = rounds // 2
    yb = n // bands
    numbers = np.arange(n)
    angles = (numbers[:, None] * numbers[None, :] % n) * (2.0 * math.pi / n)
    table = jnp.asarray(np.cos(angles) + np.sin(angles), jnp.float32)
    high, low = parts_of(table)
    left = jnp.block([[high, high], [low, low]])
    right = jnp.block([[high, low], [high, low]])
    signed = np.where(numbers < n // 2, numbers, numbers - n) * (2.0 * math.pi / n)
    screen = (4.0 * math.pi / n) ** 2
    waves = jnp.asarray(signed[:, None] ** 2 + signed[None, :] ** 2 + screen, jnp.float32)
    volume = 1.0 / n**3
    f32 = jnp.float32
    dma = pltpu.SemaphoreType.DMA
    relay = phases * 2 * half
    scratch = [
        pltpu.VMEM((slab, n, n), f32),
        pltpu.VMEM((2, grids, half, n, n), f32),
        pltpu.VMEM((relay, n, n), f32),
        pltpu.VMEM((relay, n, n), f32),
        pltpu.VMEM((phases, grids, half, n, n), f32),
        pltpu.VMEM((bands, slab, yb, n), f32),
        pltpu.VMEM((slots, n * depth, n), f32),
        pltpu.VMEM((phases, n // depth, n // 2 * depth, n), f32),
        pltpu.VMEM((phases, slots, n * depth, n), f32),
        pltpu.VMEM((grids, half, n, n), f32),
        pltpu.VMEM((2, half, n, n), f32),
        pltpu.VMEM((bands, slab, yb, n), f32),
        pltpu.VMEM((bands * bands, 8, n), f32),
        pltpu.VMEM((bands, 8, n), f32),
        pltpu.VMEM((grids, 8, n), f32),
        pltpu.VMEM((n, n), f32),
        dma((3,)),
        dma((4,)), dma((4,)),
        dma((8,)), dma((8,)),
        dma((4,)), dma((4,)),
        dma((4,)), dma((4,)),
        dma((relay,)), dma((relay,)),
        dma((relay,)), dma((relay,)),
        dma((relay,)), dma((relay,)),
        dma((2 * bands,)), dma((2 * bands,)),
        dma((phases * slots,)), dma((phases * slots,)),
        dma((phases * slots,)), dma((phases * slots,)),
        dma((half,)), dma((half,)),
        dma((half * bands,)), dma((half * bands,)),
        dma((bands,)), dma((bands,)),
        dma((grids,)), dma((grids,)),
    ]
    vmem = pl.BlockSpec(memory_space=pltpu.VMEM)
    return pl.pallas_call(
        functools.partial(whole_kernel, bands, grids, rounds, 3, 6, depth, n, volume),
        out_shape=jax.ShapeDtypeStruct((bands, slab, yb, n), f32),
        in_specs=[
            pl.BlockSpec(memory_space=pltpu.SMEM),
            pl.BlockSpec(memory_space=pl.ANY),
            vmem, vmem, vmem,
        ],
        out_specs=vmem,
        scratch_shapes=scratch,
        compiler_params=pltpu.CompilerParams(
            collective_id=0, has_side_effects=True, vmem_limit_bytes=63 * 1024 * 1024
        ),
        name="exchange",
    )(sources, orbitals, left, right, waves)


def per_device(orbitals, sources):
    held, slab, full_y, full_z = orbitals.shape
    bands = lax.axis_size("band")
    grids = lax.axis_size("grid")
    n = full_y
    rounds = sources.shape[0]
    fits = (
        held == 1 and n == full_z == slab * grids and n % 128 == 0 and slab % 32 == 0
        and grids == 4 and rounds == grids and bands % 2 == 0 and bands * bands <= n
        and n % (8 * bands) == 0 and 4 * n * n * slab * 29 <= 60 * 2**20
    )
    if fits:
        return fused(bands, grids, orbitals, sources)
    return general(orbitals, sources)


def solution(mesh):
    placed = (P("band", "grid", None, None), P())
    return jax.shard_map(
        per_device,
        mesh=mesh,
        in_specs=placed,
        out_specs=P(None, "grid", "band", None),
        check_vma=False,
    )
```

```python
import functools
import math

import jax
import jax.numpy as jnp
import numpy as np
from jax import lax
from jax.experimental import pallas as pl
from jax.experimental.pallas import tpu as pltpu
from jax.sharding import PartitionSpec as P

highest = lax.Precision.HIGHEST
MESH = pl.DeviceIdType.MESH


def spread_2(block, axis, owner):
    block = jnp.where(lax.axis_index(axis) == owner, block, jnp.zeros_like(block))
    return lax.psum(block, axis)


def cas_table(length):
    index_values = jnp.arange(length, dtype=jnp.int32)
    products = index_values[:, None] * index_values[None, :] % length
    angles = products.astype(jnp.float32) * (2.0 * math.pi / length)
    return jnp.cos(angles) + jnp.sin(angles)


def squared_waves(start, count, length):
    index_values = start + jnp.arange(count, dtype=jnp.int32)
    signed = jnp.where(index_values < length // 2, index_values, index_values - length)
    waves = signed.astype(jnp.float32) * (2.0 * math.pi / length)
    return waves * waves


def general(orbitals, sources):
    band_count, slab_x, full_y, full_z = orbitals.shape
    grid_count = lax.axis_size("grid")
    full_x = slab_x * grid_count
    total_bands = band_count * lax.axis_size("band")
    round_count = sources.shape[0]
    table_x = cas_table(full_x)
    table_y = cas_table(full_y)
    table_z = cas_table(full_z)
    column_y = full_y // grid_count
    start_y = lax.axis_index("grid") * column_y
    waves = (
        squared_waves(0, full_x, full_x)[:, None, None]
        + squared_waves(start_y, column_y, full_y)[None, :, None]
        + squared_waves(0, full_z, full_z)[None, None, :]
    )
    screen = (4.0 * math.pi / full_x) ** 2
    volume = 1.0 / (full_x * full_y * full_z)
    kernel = volume / (waves + screen)

    def plane_transform(field):
        spread = jnp.einsum("bxyz,zk->bxyk", field, table_z, precision=highest)
        return jnp.einsum("bxyk,yj->bxjk", spread, table_y, precision=highest)

    def own_slab(number):
        owner = number // band_count
        local = number % band_count
        return (owner, lax.dynamic_index_in_dim(orbitals, local, 0, keepdims=False))

    def fetch(number):
        owner, slab = own_slab(number)
        return spread_2(slab, "band", owner)

    arrived = [fetch(sources[turn]) for turn in range(round_count)]
    terms = jnp.zeros(orbitals.shape, jnp.float32)
    for turn in range(round_count):
        source = arrived[turn][None]
        spectra = plane_transform(orbitals * source)
        potential_columns = lax.all_to_all(spectra, "grid", split_axis=2, concat_axis=1, tiled=True)
        line_spread = jnp.einsum("bxyz,xa->bayz", potential_columns, table_x, precision=highest)
        line_spread = line_spread * kernel[None]
        filtered = jnp.einsum("bayz,ax->bxyz", line_spread, table_x, precision=highest)
        terms = terms + source * plane_transform(
            lax.all_to_all(filtered, "grid", split_axis=1, concat_axis=2, tiled=True)
        )
    orbital_cols, term_cols = (
        lax.all_to_all(orbitals, "band", split_axis=2, concat_axis=0, tiled=True),
        lax.all_to_all(terms, "band", split_axis=2, concat_axis=0, tiled=True),
    )
    flat_orbitals = orbital_cols.reshape(total_bands, -1)
    flat_terms = term_cols.reshape(total_bands, -1)
    partial_intersection = (
        jnp.dot(flat_orbitals, flat_terms.T, precision=highest, preferred_element_type=jnp.float32)
        * volume
    )
    intersection = lax.psum(partial_intersection, ("band", "grid"))
    factor = jnp.linalg.cholesky(intersection)
    solved = lax.linalg.triangular_solve(factor, flat_terms, left_side=True, lower=True)
    return (-solved).reshape(term_cols.shape)


def parts_of(value):
    high = value.astype(jnp.bfloat16)
    low = (value - high.astype(jnp.float32)).astype(jnp.bfloat16)
    return high, low


def along_rows(left, first, second):
    n = first.shape[0]
    h0, l0 = parts_of(first)
    h1, l1 = parts_of(second)
    right = jnp.concatenate(
        [jnp.concatenate([h0, h1], axis=1), jnp.concatenate([l0, l1], axis=1)], axis=0
    )
    both = jnp.dot(left, right, preferred_element_type=jnp.float32)
    return both[:n] + both[n:]


def along_lanes(rows, right):
    n = rows.shape[1]
    high, low = parts_of(rows)
    both = jnp.dot(
        jnp.concatenate([high, low], axis=1), right, preferred_element_type=jnp.float32
    )
    return both[:, :n] + both[:, n:]


def pick(i, values):
    out = values[-1]
    for m in reversed(range(len(values) - 1)):
        out = jnp.where(i == m, values[m], out)
    return out


def whole_kernel(
    bands, grids, rounds, ahead, early, depth, n, volume,
    sources, orbitals, left_ref, right_ref, waves_ref, out, *scratch,
):
    (own, orb, up, dn, src, fcol, spec, cols, back, terms, pin, tcol, part, sums_b, sums_g, splat,
     in_sem, m_send, m_recv, ox_send, ox_recv, oy_send, oy_recv, or_send, or_recv,
     up_send, up_recv, dn_send, dn_recv, y_send, y_recv, o_send, o_recv, f_send, f_recv,
     b_send, b_recv, p_send, p_recv, t_send, t_recv,
     sb_send, sb_recv, sg_send, sg_recv) = scratch
    b = lax.axis_index("band")
    g = lax.axis_index("grid")
    nz = bands // 2
    z, core = b // 2, b % 2
    slab = n // grids
    half = slab // 2
    yb = n // bands
    pieces = half // depth
    slots = grids * pieces
    quarter = half // 4
    pair = 2
    pairs = half // pair
    mine = n // 2 * depth
    phases = rounds // 2
    total_units = phases * 2 * half
    lag = (nz - 1) * ahead
    partner = z * 2 + (1 - core)
    gx = g + 1 - 2 * (g % 2)
    gy = lax.rem(g + 2, grids)
    gd = gx + 2 - 4 * (gx // 2)
    column, row = g % 2, g // 2

    barrier = pltpu.get_barrier_semaphore()
    for d in range(1, bands):
        pl.semaphore_signal(barrier, inc=1, device_id=(lax.rem(b + d, bands), g), device_id_type=MESH)
    for d in range(bands):
        pl.semaphore_signal(barrier, inc=1, device_id=(lax.rem(b + d, bands), gy), device_id_type=MESH)
    pl.semaphore_signal(barrier, inc=1, device_id=(b, gx), device_id_type=MESH)
    pl.semaphore_signal(barrier, inc=1, device_id=(b, gd), device_id_type=MESH)
    loads = [
        pltpu.make_async_copy(
            orbitals.at[0, pl.ds((1 - core) * half, half)], own.at[pl.ds((1 - core) * half, half)],
            in_sem.at[0],
        ),
        pltpu.make_async_copy(
            orbitals.at[0, pl.ds(core * half, half)], orb.at[core, g], in_sem.at[1]
        ),
        pltpu.make_async_copy(
            orbitals.at[0, pl.ds(core * half, half)], own.at[pl.ds(core * half, half)], in_sem.at[2]
        ),
    ]
    for load in loads:
        load.start()
    for load in loads:
        load.wait()
    pl.semaphore_wait(barrier, 2 * bands + 1)

    def mate_copy(u, parity):
        return pltpu.make_async_remote_copy(
            src_ref=own.at[pl.ds((1 - core) * half + u * quarter, quarter)],
            dst_ref=orb.at[parity, g, pl.ds(u * quarter, quarter)],
            send_sem=m_send.at[u], recv_sem=m_recv.at[u],
            device_id=(partner, g), device_id_type=MESH,
        )

    def ox_copy(u, which, owner):
        block = orb.at[which, owner, pl.ds(u * quarter, quarter)]
        return pltpu.make_async_remote_copy(
            src_ref=block, dst_ref=block,
            send_sem=ox_send.at[2 * u + which], recv_sem=ox_recv.at[2 * u + which],
            device_id=(b, gx), device_id_type=MESH,
        )

    def oy_copy(u, which, owner):
        block = orb.at[which, owner, pl.ds(u * quarter, quarter)]
        return pltpu.make_async_remote_copy(
            src_ref=block, dst_ref=block,
            send_sem=oy_send.at[u], recv_sem=oy_recv.at[u],
            device_id=(b, gy), device_id_type=MESH,
        )

    def or_copy(u, owner):
        block = orb.at[row, owner, pl.ds(u * quarter, quarter)]
        return pltpu.make_async_remote_copy(
            src_ref=block, dst_ref=block,
            send_sem=or_send.at[u], recv_sem=or_recv.at[u],
            device_id=(b, gx), device_id_type=MESH,
        )

    def up_copy(v):
        return pltpu.make_async_remote_copy(
            src_ref=up.at[v], dst_ref=up.at[v],
            send_sem=up_send.at[v], recv_sem=up_recv.at[v],
            device_id=(lax.rem(b + 2, bands), g), device_id_type=MESH,
        )

    def dn_copy(v):
        return pltpu.make_async_remote_copy(
            src_ref=dn.at[v], dst_ref=dn.at[v],
            send_sem=dn_send.at[v], recv_sem=dn_recv.at[v],
            device_id=(lax.rem(b + bands - 2, bands), g), device_id_type=MESH,
        )

    def place(v):
        q = lax.div(v, 2 * half)
        side = lax.rem(lax.div(v, half), 2)
        return q, side, lax.rem(v, half)

    def y_copy(v, near, far):
        q, side, u = place(v)
        block = src.at[q, jnp.where(side == 0, near, far), u]
        return pltpu.make_async_remote_copy(
            src_ref=block, dst_ref=block,
            send_sem=y_send.at[v], recv_sem=y_recv.at[v],
            device_id=(b, gy), device_id_type=MESH,
        )

    def o_copy(target, owner, late):
        planes = pl.ds(early, slab - early) if late else pl.ds(0, early)
        return pltpu.make_async_remote_copy(
            src_ref=own.at[planes, pl.ds(target * yb, yb)], dst_ref=fcol.at[owner, planes],
            send_sem=o_send.at[late * bands + target], recv_sem=o_recv.at[late * bands + owner],
            device_id=(target, g), device_id_type=MESH,
        )

    for u in range(4):
        mate_copy(u, core).start()
    for d in range(1, bands):
        o_copy(lax.rem(b + d, bands), b, 0).start()
    for u in range(4):
        mate_copy(u, 1 - core).wait_recv()
        oy_copy(u, 1 - row, g).start()
        for which in range(2):
            ox_copy(u, which, g).start()

    def step(t, _):
        @pl.when(jnp.logical_and(t >= half, jnp.logical_and(t < 2 * half, lax.rem(t, quarter) == 0)))
        def _():
            u = lax.div(t - half, quarter)
            for which in range(2):
                ox_copy(u, which, gx).wait_recv()

        for u in range(4):
            @pl.when(t == quarter * (u + 1) + 3)
            def _():
                oy_copy(u, row, gy).wait_recv()
                or_copy(u, gy).start()

        def pass_on(v, box, copy, first, last):
            @pl.when(jnp.logical_and(v >= 0, v < total_units))
            def _():
                q, side, u = place(v)
                s = sources[phases * column + q]
                at = jnp.where(side == 0, g, gx)
                here = jnp.where(lax.rem(s, 2) == 0, orb[0, at, u], orb[1, at, u])

                @pl.when(first)
                def _():
                    box[v] = here

                @pl.when(jnp.logical_not(first))
                def _():
                    copy(v).wait_recv()
                    box[v] = jnp.where(lax.div(s, 2) == z, here, box[v])

                @pl.when(jnp.logical_not(last))
                def _():
                    copy(v).start()

        pass_on(t - z * ahead, up, up_copy, z == 0, z == nz - 1)
        pass_on(t - (nz - 1 - z) * ahead, dn, dn_copy, z == nz - 1, z == 0)
        v = t - lag

        @pl.when(jnp.logical_and(v >= 0, v < total_units))
        def _():
            q, side, u = place(v)
            s = sources[phases * column + q]
            src[q, jnp.where(side == 0, g, gx), u] = jnp.where(s < 2 * z + 2, up[v], dn[v])
            y_copy(v, g, gx).start()

        return 0

    left = left_ref[...]
    right = right_ref[...]
    base = waves_ref[...]

    def f_copy(q, at, piece, side):
        slot = at * pieces + piece
        return pltpu.make_async_remote_copy(
            src_ref=spec.at[slot, pl.ds((1 - core) * mine, mine)],
            dst_ref=cols.at[q, (at * 2 + side) * pieces + piece],
            send_sem=f_send.at[q * slots + slot], recv_sem=f_recv.at[q * slots + slot],
            device_id=(partner, g), device_id_type=MESH,
        )

    def b_copy(q, at, piece, side):
        slot = at * pieces + piece
        return pltpu.make_async_remote_copy(
            src_ref=cols.at[q, (at * 2 + 1 - side) * pieces + piece],
            dst_ref=back.at[q, slot, pl.ds(side * mine, mine)],
            send_sem=b_send.at[q * slots + slot], recv_sem=b_recv.at[q * slots + slot],
            device_id=(partner, g), device_id_type=MESH,
        )

    order = [(g, 0), (g, 1), (gy, 0), (gx, 0), (gy, 1), (gx, 1), (gd, 0), (gd, 1)]

    def forward(q, i):
        at = pick(i, [a for a, _ in order])
        piece = pick(i, [p for _, p in order])
        far = at == gd

        @pl.when(jnp.logical_or(far, at == gy))
        def _():
            start = q * 2 * half + jnp.where(far, half, 0) + piece * depth

            def arrive(e, _):
                y_copy(start + e, gy, gd).wait_recv()
                return 0

            lax.fori_loop(0, depth, arrive, 0)

        if q == 0:
            @pl.when(far)
            def _():
                for e in range(2):
                    or_copy(2 * piece + e, gd).wait_recv()

        slot = at * pieces + piece
        if q > 0:
            f_copy(q - 1, at, piece, core).wait_send()
        for k in range(0, depth, 2):
            here = pl.ds(piece * depth + k, 2)
            pair = src[q, at, here] * orb[row, at, here]
            rows = along_lanes(pair.reshape(2 * n, n), right)
            planes = along_rows(left, rows[:n], rows[n:])
            spec[slot, pl.ds(k, n, stride=depth), :] = planes[:, :n]
            spec[slot, pl.ds(k + 1, n, stride=depth), :] = planes[:, n:]
        f_copy(q, at, piece, core).start()
        cols[q, (at * 2 + core) * pieces + piece] = spec[slot, pl.ds(core * mine, mine), :]

    def every(q, copy_of):
        for at in range(grids):
            for piece in range(pieces):
                copy_of(q, at, piece)

    lines_count = n // 4

    def lines(q, first, count):
        def line(k):
            held = [
                cols[q, :, pl.ds(pl.multiple_of((2 * k + e) * depth, depth), depth), :].reshape(n, n)
                for e in range(2)
            ]
            moved = along_rows(left, held[0], held[1])
            filtered = []
            for e in range(2):
                ky = core * (n // 2) + 2 * k + e
                signed = jnp.where(ky < n // 2, ky, ky - n).astype(jnp.float32)
                wave = signed * (2.0 * math.pi / n)
                filtered.append(moved[:, e * n:(e + 1) * n] * (volume / (base + wave * wave)))
            done = along_rows(left, filtered[0], filtered[1])
            for e in range(2):
                cols[q, :, pl.ds(pl.multiple_of((2 * k + e) * depth, depth), depth), :] = (
                    done[:, e * n:(e + 1) * n].reshape(n // depth, depth, n)
                )

        def group(i, _):
            for e in range(2):
                line(first + 2 * i + e)
            return 0

        lax.fori_loop(0, count // 2, group, 0)

    def inverse(q, at, piece):
        slot = at * pieces + piece
        b_copy(q, at, piece, 1 - core).wait_recv()
        back[q, slot, pl.ds(core * mine, mine), :] = cols[q, (at * 2 + core) * pieces + piece]
        for k in range(0, depth, 2):
            planes = along_rows(
                left,
                back[q, slot, pl.ds(k, n, stride=depth), :],
                back[q, slot, pl.ds(k + 1, n, stride=depth), :],
            )
            rows = jnp.concatenate([planes[:, :n], planes[:, n:]], axis=0)
            potential = along_lanes(rows, right).reshape(2, n, n)
            here = pl.ds(piece * depth + k, 2)
            value = src[q, at, here] * potential
            if q == 0:
                terms[at, here] = value
            else:
                terms[at, here] += value

    def p_copy(at, side, m):
        return pltpu.make_async_remote_copy(
            src_ref=terms.at[at, pl.ds(m * pair, pair)],
            dst_ref=pin.at[side, pl.ds(m * pair, pair)],
            send_sem=p_send.at[side * pairs + m], recv_sem=p_recv.at[side * pairs + m],
            device_id=(b, gx), device_id_type=MESH,
        )

    def bounds(q, remote):
        local = [q * 2 * half + lag + side * half + (p + 1) * depth for side in range(2) for p in range(2)]
        far = [at + remote for at in local]
        last = [far[2] + 6, far[3] + 1] if q == 0 else far[2:]
        return [local[0], local[1], far[0], local[2], far[1], local[3], *last]

    first_bounds = bounds(0, 10)
    second_bounds = bounds(1, 10)

    def advance(start, stop):
        lax.fori_loop(start, stop, step, 0)

    def first_forward(i, at):
        stop = pick(i, first_bounds)
        advance(at, stop)
        forward(0, i)
        return stop

    at = lax.fori_loop(0, slots, first_forward, 0)
    advance(first_bounds[-1], first_bounds[-1] + 2)
    every(0, lambda q, at, piece: f_copy(q, at, piece, 1 - core).wait_recv())
    settle = first_bounds[-1] + 2

    def first_lines(i, _):
        lines(0, i * (lines_count // slots), lines_count // slots)
        advance(settle + i, settle + i + 1)
        return 0

    lax.fori_loop(0, slots, first_lines, 0)
    every(0, lambda q, at, piece: b_copy(q, at, piece, core).start())
    reached = settle + slots

    def second_forward(i, at):
        stop = jnp.maximum(pick(i, second_bounds), reached + 2 * (i + 1))
        middle = jnp.minimum(at + 1, stop)
        advance(at, middle)
        inverse(0, lax.div(i, pieces), lax.rem(i, pieces))
        advance(middle, stop)
        forward(1, i)

        @pl.when(i == 5)
        def _():
            for d in range(1, bands):
                o_copy(lax.rem(b + d, bands), b, 1).start()

        return stop

    lax.fori_loop(0, slots, second_forward, reached)
    every(1, lambda q, at, piece: f_copy(q, at, piece, 1 - core).wait_recv())
    lines(1, 0, lines_count)
    for at in (gd, gx, gy, g):
        for piece in range(pieces):
            b_copy(1, at, piece, core).start()

    fcol[b] = own[:, pl.ds(b * yb, yb), :]
    part[...] = jnp.zeros_like(part)

    def second_inverse(i, _):
        at = pick(lax.div(i, pieces), [gd, gx, gy, g])
        piece = lax.rem(i, pieces)
        inverse(1, at, piece)

        @pl.when(i < 2 * pieces)
        def _():
            for e in range(depth // pair):
                p_copy(at, lax.div(i, pieces), depth // pair * piece + e).start()

        return 0

    lax.fori_loop(0, slots, second_inverse, 0)

    orbital = 2 * z + row

    wait = 3
    def t_copy(m, at, target):
        rows = pl.ds(m * pair, pair)
        return pltpu.make_async_remote_copy(
            src_ref=terms.at[at, rows, pl.ds(target * yb, yb)],
            dst_ref=tcol.at[orbital, pl.ds(core * half + m * pair, pair)],
            send_sem=t_send.at[(jnp.where(at == g, 1, 0) * pairs + m) * bands + target],
            recv_sem=t_recv.at[(orbital * 2 + core) * pairs + m],
            device_id=(target, at), device_id_type=MESH,
        )

    def t_arrival(m, which, side):
        block = tcol.at[which, pl.ds(side * half + m * pair, pair)]
        return pltpu.make_async_remote_copy(
            src_ref=block, dst_ref=block,
            send_sem=t_send.at[0], recv_sem=t_recv.at[(which * 2 + side) * pairs + m],
            device_id=(partner, g), device_id_type=MESH,
        )

    def finish(i, _):
        @pl.when(i < 2 * pairs)
        def _():
            own_side = lax.div(i, pairs)
            m = lax.rem(i, pairs)
            at = jnp.where(own_side == 0, gy, g)
            rows = pl.ds(m * pair, pair)
            p_copy(at, own_side, m).wait_recv()
            terms[at, rows] += pin[own_side, rows]

            @pl.when(own_side == 0)
            def _():
                for target in range(bands):
                    t_copy(m, gy, target).start()

            @pl.when(own_side == 1)
            def _():
                for d in range(1, bands):
                    t_copy(m, g, lax.rem(b + d, bands)).start()
                tcol[orbital, pl.ds(core * half + m * pair, pair)] = terms[
                    g, rows, pl.ds(b * yb, yb), :
                ]

        @pl.when(i == wait)
        def _():
            for d in range(1, bands):
                for late in range(2):
                    o_copy(b, lax.rem(b + d, bands), late).wait_recv()

        @pl.when(i >= wait)
        def _():
            own_side = lax.div(i - wait, pairs)
            m = lax.rem(i - wait, pairs)
            parity = jnp.where(own_side == 0, 1 - row, row)
            for k in range(nz):
                for side in range(2):
                    local = jnp.logical_and(
                        jnp.logical_and(own_side == 1, z == k), core == side
                    )

                    @pl.when(jnp.logical_not(local))
                    def _():
                        t_arrival(m, 2 * k + parity, side).wait_recv()

            def one(a, _):
                held = [fcol[a, pl.ds(side * half + m * pair, pair)] for side in range(2)]
                for k in range(nz):
                    which = 2 * k + parity
                    total = jnp.zeros((8, n), jnp.float32)
                    for side in range(2):
                        prod = held[side] * tcol[which, pl.ds(side * half + m * pair, pair)]
                        total = total + jnp.sum(prod.reshape(-1, 8, n), axis=0)
                    part[a * bands + which] += total
                return 0

            lax.fori_loop(0, bands, one, 0)

        return 0

    lax.fori_loop(0, 2 * pairs + wait, finish, 0)

    count = bands * bands
    flat = jnp.sum(part[...], axis=1)
    if count < n:
        flat = jnp.concatenate([flat, jnp.zeros((n - count, n), jnp.float32)], axis=0)
    lanes = jnp.sum(flat.T, axis=0, keepdims=True)
    sums_b[b] = jnp.broadcast_to(lanes, (8, n))

    def sb_copy(target, owner):
        return pltpu.make_async_remote_copy(
            src_ref=sums_b.at[b], dst_ref=sums_b.at[owner],
            send_sem=sb_send.at[target], recv_sem=sb_recv.at[owner],
            device_id=(target, g), device_id_type=MESH,
        )

    def sg_copy(target, owner):
        return pltpu.make_async_remote_copy(
            src_ref=sums_g.at[g], dst_ref=sums_g.at[owner],
            send_sem=sg_send.at[target], recv_sem=sg_recv.at[owner],
            device_id=(b, target), device_id_type=MESH,
        )

    for d in range(1, bands):
        sb_copy(lax.rem(b + d, bands), b).start()
    for d in range(1, bands):
        sb_copy(b, lax.rem(b + d, bands)).wait_recv()
    sums_g[g] = jnp.sum(sums_b[...], axis=0)
    for d in range(1, grids):
        sg_copy(lax.rem(g + d, grids), g).start()
    for d in range(1, grids):
        sg_copy(g, lax.rem(g + d, grids)).wait_recv()
    total = jnp.sum(sums_g[...], axis=0)[:1] * volume
    splat[...] = jnp.broadcast_to(total, (n, n)).T

    def entry(i, k):
        first = splat[pl.ds(i * bands + k, 1), :]
        return 0.5 * (first + splat[pl.ds(k * bands + i, 1), :])

    factor = {}
    inverse_diag = {}
    for k in range(bands):
        diag = entry(k, k)
        for m in range(k):
            diag = diag - factor[k, m] * factor[k, m]
        inverse_diag[k] = 1.0 / jnp.sqrt(diag)
        for i in range(k + 1, bands):
            value = entry(i, k)
            for m in range(k):
                value = value - factor[i, m] * factor[k, m]
            factor[i, k] = value * inverse_diag[k]
    for k in range(bands):
        splat[pl.ds(k * bands + k, 1), :] = inverse_diag[k]
        for i in range(k + 1, bands):
            splat[pl.ds(i * bands + k, 1), :] = factor[i, k]

    def solve(p, _):
        x = pl.ds(4 * p, 4)
        solved = []
        for i in range(bands):
            value = -tcol[i, x]
            for k in range(i):
                value = value - splat[pl.ds(i * bands + k, 1), :] * solved[k]
            value = value * splat[pl.ds(i * bands + i, 1), :]
            out[i, x] = value
            solved.append(value)
        return 0

    lax.fori_loop(0, slab // 4, solve, 0)

    for u in range(4):
        mate_copy(u, core).wait_send()
        oy_copy(u, 1 - row, g).wait_send()
        or_copy(u, gy).wait_send()
        for which in range(2):
            ox_copy(u, which, g).wait_send()

    def settle_units(v, _):
        @pl.when(z < nz - 1)
        def _():
            up_copy(v).wait_send()

        @pl.when(z > 0)
        def _():
            dn_copy(v).wait_send()

        y_copy(v, g, gx).wait_send()
        return 0

    lax.fori_loop(0, total_units, settle_units, 0)
    every(phases - 1, lambda q, at, piece: f_copy(q, at, piece, core).wait_send())
    for q in range(phases):
        every(q, lambda q, at, piece: b_copy(q, at, piece, core).wait_send())
    for m in range(pairs):
        p_copy(gd, 0, m).wait_send()
        p_copy(gx, 1, m).wait_send()
        for target in range(bands):
            t_copy(m, gy, target).wait_send()
        for d in range(1, bands):
            t_copy(m, g, lax.rem(b + d, bands)).wait_send()
    for d in range(1, bands):
        for late in range(2):
            o_copy(lax.rem(b + d, bands), b, late).wait_send()
        sb_copy(lax.rem(b + d, bands), b).wait_send()
    for d in range(1, grids):
        sg_copy(lax.rem(g + d, grids), g).wait_send()


def fused(bands, grids, orbitals, sources):
    n = orbitals.shape[2]
    rounds = sources.shape[0]
    slab = n // grids
    half = slab // 2
    depth = 8
    pieces = half // depth
    slots = grids * pieces
    phases = rounds // 2
    yb = n // bands
    numbers = np.arange(n)
    angles = (numbers[:, None] * numbers[None, :] % n) * (2.0 * math.pi / n)
    table = jnp.asarray(np.cos(angles) + np.sin(angles), jnp.float32)
    high, low = parts_of(table)
    left = jnp.block([[high, high], [low, low]])
    right = jnp.block([[high, low], [high, low]])
    signed = np.where(numbers < n // 2, numbers, numbers - n) * (2.0 * math.pi / n)
    screen = (4.0 * math.pi / n) ** 2
    waves = jnp.asarray(signed[:, None] ** 2 + signed[None, :] ** 2 + screen, jnp.float32)
    volume = 1.0 / n**3
    f32 = jnp.float32
    dma = pltpu.SemaphoreType.DMA
    relay = phases * 2 * half
    scratch = [
        pltpu.VMEM((slab, n, n), f32),
        pltpu.VMEM((2, grids, half, n, n), f32),
        pltpu.VMEM((relay, n, n), f32),
        pltpu.VMEM((relay, n, n), f32),
        pltpu.VMEM((phases, grids, half, n, n), f32),
        pltpu.VMEM((bands, slab, yb, n), f32),
        pltpu.VMEM((slots, n * depth, n), f32),
        pltpu.VMEM((phases, n // depth, n // 2 * depth, n), f32),
        pltpu.VMEM((phases, slots, n * depth, n), f32),
        pltpu.VMEM((grids, half, n, n), f32),
        pltpu.VMEM((2, half, n, n), f32),
        pltpu.VMEM((bands, slab, yb, n), f32),
        pltpu.VMEM((bands * bands, 8, n), f32),
        pltpu.VMEM((bands, 8, n), f32),
        pltpu.VMEM((grids, 8, n), f32),
        pltpu.VMEM((n, n), f32),
        dma((3,)),
        dma((4,)), dma((4,)),
        dma((8,)), dma((8,)),
        dma((4,)), dma((4,)),
        dma((4,)), dma((4,)),
        dma((relay,)), dma((relay,)),
        dma((relay,)), dma((relay,)),
        dma((relay,)), dma((relay,)),
        dma((2 * bands,)), dma((2 * bands,)),
        dma((phases * slots,)), dma((phases * slots,)),
        dma((phases * slots,)), dma((phases * slots,)),
        dma((half,)), dma((half,)),
        dma((half * bands,)), dma((half * bands,)),
        dma((bands,)), dma((bands,)),
        dma((grids,)), dma((grids,)),
    ]
    vmem = pl.BlockSpec(memory_space=pltpu.VMEM)
    return pl.pallas_call(
        functools.partial(whole_kernel, bands, grids, rounds, 3, 6, depth, n, volume),
        out_shape=jax.ShapeDtypeStruct((bands, slab, yb, n), f32),
        in_specs=[
            pl.BlockSpec(memory_space=pltpu.SMEM),
            pl.BlockSpec(memory_space=pl.ANY),
            vmem, vmem, vmem,
        ],
        out_specs=vmem,
        scratch_shapes=scratch,
        compiler_params=pltpu.CompilerParams(
            collective_id=0, has_side_effects=True, vmem_limit_bytes=63 * 1024 * 1024
        ),
        name="exchange",
    )(sources, orbitals, left, right, waves)


def per_device(orbitals, sources):
    held, slab, full_y, full_z = orbitals.shape
    bands = lax.axis_size("band")
    grids = lax.axis_size("grid")
    n = full_y
    rounds = sources.shape[0]
    fits = (
        held == 1 and n == full_z == slab * grids and n % 128 == 0 and slab % 32 == 0
        and grids == 4 and rounds == grids and bands % 2 == 0 and bands * bands <= n
        and n % (8 * bands) == 0 and 4 * n * n * slab * 29 <= 60 * 2**20
    )
    if fits:
        return fused(bands, grids, orbitals, sources)
    return general(orbitals, sources)


def solution(mesh):
    placed = (P("band", "grid", None, None), P())
    return jax.shard_map(
        per_device,
        mesh=mesh,
        in_specs=placed,
        out_specs=P(None, "grid", "band", None),
        check_vma=False,
    )
```

```python
import functools
import math

import jax
import jax.numpy as jnp
import numpy as np
from jax import lax
from jax.experimental import pallas as pl
from jax.experimental.pallas import tpu as pltpu
from jax.sharding import PartitionSpec as P

highest = lax.Precision.HIGHEST
MESH = pl.DeviceIdType.MESH


def spread_2(block, axis, owner):
    block = jnp.where(lax.axis_index(axis) == owner, block, jnp.zeros_like(block))
    return lax.psum(block, axis)


def cas_table(length):
    index_values = jnp.arange(length, dtype=jnp.int32)
    products = index_values[:, None] * index_values[None, :] % length
    angles = products.astype(jnp.float32) * (2.0 * math.pi / length)
    return jnp.cos(angles) + jnp.sin(angles)


def squared_waves(start, count, length):
    index_values = start + jnp.arange(count, dtype=jnp.int32)
    signed = jnp.where(index_values < length // 2, index_values, index_values - length)
    waves = signed.astype(jnp.float32) * (2.0 * math.pi / length)
    return waves * waves


def general(orbitals, sources):
    band_count, slab_x, full_y, full_z = orbitals.shape
    grid_count = lax.axis_size("grid")
    full_x = slab_x * grid_count
    total_bands = band_count * lax.axis_size("band")
    round_count = sources.shape[0]
    table_x = cas_table(full_x)
    table_y = cas_table(full_y)
    table_z = cas_table(full_z)
    column_y = full_y // grid_count
    start_y = lax.axis_index("grid") * column_y
    waves = (
        squared_waves(0, full_x, full_x)[:, None, None]
        + squared_waves(start_y, column_y, full_y)[None, :, None]
        + squared_waves(0, full_z, full_z)[None, None, :]
    )
    screen = (4.0 * math.pi / full_x) ** 2
    volume = 1.0 / (full_x * full_y * full_z)
    kernel = volume / (waves + screen)

    def plane_transform(field):
        spread = jnp.einsum("bxyz,zk->bxyk", field, table_z, precision=highest)
        return jnp.einsum("bxyk,yj->bxjk", spread, table_y, precision=highest)

    def own_slab(number):
        owner = number // band_count
        local = number % band_count
        return (owner, lax.dynamic_index_in_dim(orbitals, local, 0, keepdims=False))

    def fetch(number):
        owner, slab = own_slab(number)
        return spread_2(slab, "band", owner)

    arrived = [fetch(sources[turn]) for turn in range(round_count)]
    terms = jnp.zeros(orbitals.shape, jnp.float32)
    for turn in range(round_count):
        source = arrived[turn][None]
        spectra = plane_transform(orbitals * source)
        potential_columns = lax.all_to_all(spectra, "grid", split_axis=2, concat_axis=1, tiled=True)
        line_spread = jnp.einsum("bxyz,xa->bayz", potential_columns, table_x, precision=highest)
        line_spread = line_spread * kernel[None]
        filtered = jnp.einsum("bayz,ax->bxyz", line_spread, table_x, precision=highest)
        terms = terms + source * plane_transform(
            lax.all_to_all(filtered, "grid", split_axis=1, concat_axis=2, tiled=True)
        )
    orbital_cols, term_cols = (
        lax.all_to_all(orbitals, "band", split_axis=2, concat_axis=0, tiled=True),
        lax.all_to_all(terms, "band", split_axis=2, concat_axis=0, tiled=True),
    )
    flat_orbitals = orbital_cols.reshape(total_bands, -1)
    flat_terms = term_cols.reshape(total_bands, -1)
    partial_intersection = (
        jnp.dot(flat_orbitals, flat_terms.T, precision=highest, preferred_element_type=jnp.float32)
        * volume
    )
    intersection = lax.psum(partial_intersection, ("band", "grid"))
    factor = jnp.linalg.cholesky(intersection)
    solved = lax.linalg.triangular_solve(factor, flat_terms, left_side=True, lower=True)
    return (-solved).reshape(term_cols.shape)


def parts_of(value):
    high = value.astype(jnp.bfloat16)
    low = (value - high.astype(jnp.float32)).astype(jnp.bfloat16)
    return high, low


def along_rows(left, first, second):
    n = first.shape[0]
    h0, l0 = parts_of(first)
    h1, l1 = parts_of(second)
    right = jnp.concatenate(
        [jnp.concatenate([h0, h1], axis=1), jnp.concatenate([l0, l1], axis=1)], axis=0
    )
    both = jnp.dot(left, right, preferred_element_type=jnp.float32)
    return both[:n] + both[n:]


def along_lanes(rows, right):
    n = rows.shape[1]
    high, low = parts_of(rows)
    both = jnp.dot(
        jnp.concatenate([high, low], axis=1), right, preferred_element_type=jnp.float32
    )
    return both[:, :n] + both[:, n:]


def pick(i, values):
    out = values[-1]
    for m in reversed(range(len(values) - 1)):
        out = jnp.where(i == m, values[m], out)
    return out


def whole_kernel(
    bands, grids, rounds, ahead, early, depth, n, volume,
    sources, orbitals, left_ref, right_ref, waves_ref, out, *scratch,
):
    (own, orb, up, dn, src, fcol, spec, cols, back, terms, pin, tcol, held_out, part, sums_b, sums_g, splat,
     in_sem, m_send, m_recv, ox_send, ox_recv, oy_send, oy_recv, or_send, or_recv,
     up_send, up_recv, dn_send, dn_recv, y_send, y_recv, o_send, o_recv, f_send, f_recv,
     b_send, b_recv, p_send, p_recv, t_send, t_recv,
     sb_send, sb_recv, sg_send, sg_recv, out_sem) = scratch
    b = lax.axis_index("band")
    g = lax.axis_index("grid")
    nz = bands // 2
    z, core = b // 2, b % 2
    slab = n // grids
    half = slab // 2
    yb = n // bands
    pieces = half // depth
    slots = grids * pieces
    quarter = half // 4
    pair = 2
    pairs = half // pair
    mine = n // 2 * depth
    phases = rounds // 2
    total_units = phases * 2 * half
    lag = (nz - 1) * ahead
    partner = z * 2 + (1 - core)
    gx = g + 1 - 2 * (g % 2)
    gy = lax.rem(g + 2, grids)
    gd = gx + 2 - 4 * (gx // 2)
    column, row = g % 2, g // 2

    barrier = pltpu.get_barrier_semaphore()
    for d in range(1, bands):
        pl.semaphore_signal(barrier, inc=1, device_id=(lax.rem(b + d, bands), g), device_id_type=MESH)
    for d in range(bands):
        pl.semaphore_signal(barrier, inc=1, device_id=(lax.rem(b + d, bands), gy), device_id_type=MESH)
    pl.semaphore_signal(barrier, inc=1, device_id=(b, gx), device_id_type=MESH)
    pl.semaphore_signal(barrier, inc=1, device_id=(b, gd), device_id_type=MESH)
    loads = [
        pltpu.make_async_copy(
            orbitals.at[0, pl.ds((1 - core) * half, half)], own.at[pl.ds((1 - core) * half, half)],
            in_sem.at[0],
        ),
        pltpu.make_async_copy(
            orbitals.at[0, pl.ds(core * half, half)], orb.at[core, g], in_sem.at[1]
        ),
        pltpu.make_async_copy(
            orbitals.at[0, pl.ds(core * half, half)], own.at[pl.ds(core * half, half)], in_sem.at[2]
        ),
    ]
    for load in loads:
        load.start()
    for load in loads:
        load.wait()
    pl.semaphore_wait(barrier, 2 * bands + 1)

    def mate_copy(u, parity):
        return pltpu.make_async_remote_copy(
            src_ref=own.at[pl.ds((1 - core) * half + u * quarter, quarter)],
            dst_ref=orb.at[parity, g, pl.ds(u * quarter, quarter)],
            send_sem=m_send.at[u], recv_sem=m_recv.at[u],
            device_id=(partner, g), device_id_type=MESH,
        )

    def ox_copy(u, which, owner):
        block = orb.at[which, owner, pl.ds(u * quarter, quarter)]
        return pltpu.make_async_remote_copy(
            src_ref=block, dst_ref=block,
            send_sem=ox_send.at[2 * u + which], recv_sem=ox_recv.at[2 * u + which],
            device_id=(b, gx), device_id_type=MESH,
        )

    def oy_copy(u, which, owner):
        block = orb.at[which, owner, pl.ds(u * quarter, quarter)]
        return pltpu.make_async_remote_copy(
            src_ref=block, dst_ref=block,
            send_sem=oy_send.at[u], recv_sem=oy_recv.at[u],
            device_id=(b, gy), device_id_type=MESH,
        )

    def or_copy(u, owner):
        block = orb.at[row, owner, pl.ds(u * quarter, quarter)]
        return pltpu.make_async_remote_copy(
            src_ref=block, dst_ref=block,
            send_sem=or_send.at[u], recv_sem=or_recv.at[u],
            device_id=(b, gx), device_id_type=MESH,
        )

    def up_copy(v):
        return pltpu.make_async_remote_copy(
            src_ref=up.at[v], dst_ref=up.at[v],
            send_sem=up_send.at[v], recv_sem=up_recv.at[v],
            device_id=(lax.rem(b + 2, bands), g), device_id_type=MESH,
        )

    def dn_copy(v):
        return pltpu.make_async_remote_copy(
            src_ref=dn.at[v], dst_ref=dn.at[v],
            send_sem=dn_send.at[v], recv_sem=dn_recv.at[v],
            device_id=(lax.rem(b + bands - 2, bands), g), device_id_type=MESH,
        )

    def place(v):
        q = lax.div(v, 2 * half)
        side = lax.rem(lax.div(v, half), 2)
        return q, side, lax.rem(v, half)

    def y_copy(v, near, far):
        q, side, u = place(v)
        block = src.at[q, jnp.where(side == 0, near, far), u]
        return pltpu.make_async_remote_copy(
            src_ref=block, dst_ref=block,
            send_sem=y_send.at[v], recv_sem=y_recv.at[v],
            device_id=(b, gy), device_id_type=MESH,
        )

    def o_copy(target, owner, late):
        planes = pl.ds(early, slab - early) if late else pl.ds(0, early)
        return pltpu.make_async_remote_copy(
            src_ref=own.at[planes, pl.ds(target * yb, yb)], dst_ref=fcol.at[owner, planes],
            send_sem=o_send.at[late * bands + target], recv_sem=o_recv.at[late * bands + owner],
            device_id=(target, g), device_id_type=MESH,
        )

    for u in range(4):
        mate_copy(u, core).start()
    for d in range(1, bands):
        o_copy(lax.rem(b + d, bands), b, 0).start()
    for u in range(4):
        mate_copy(u, 1 - core).wait_recv()
        oy_copy(u, 1 - row, g).start()
        for which in range(2):
            ox_copy(u, which, g).start()

    def step(t, _):
        @pl.when(jnp.logical_and(t >= half, jnp.logical_and(t < 2 * half, lax.rem(t, quarter) == 0)))
        def _():
            u = lax.div(t - half, quarter)
            for which in range(2):
                ox_copy(u, which, gx).wait_recv()

        for u in range(4):
            @pl.when(t == quarter * (u + 1) + 3)
            def _():
                oy_copy(u, row, gy).wait_recv()
                or_copy(u, gy).start()

        def pass_on(v, box, copy, first, last):
            @pl.when(jnp.logical_and(v >= 0, v < total_units))
            def _():
                q, side, u = place(v)
                s = sources[phases * column + q]
                at = jnp.where(side == 0, g, gx)
                here = jnp.where(lax.rem(s, 2) == 0, orb[0, at, u], orb[1, at, u])

                @pl.when(first)
                def _():
                    box[v] = here

                @pl.when(jnp.logical_not(first))
                def _():
                    copy(v).wait_recv()
                    box[v] = jnp.where(lax.div(s, 2) == z, here, box[v])

                @pl.when(jnp.logical_not(last))
                def _():
                    copy(v).start()

        pass_on(t - z * ahead, up, up_copy, z == 0, z == nz - 1)
        pass_on(t - (nz - 1 - z) * ahead, dn, dn_copy, z == nz - 1, z == 0)
        v = t - lag

        @pl.when(jnp.logical_and(v >= 0, v < total_units))
        def _():
            q, side, u = place(v)
            s = sources[phases * column + q]
            src[q, jnp.where(side == 0, g, gx), u] = jnp.where(s < 2 * z + 2, up[v], dn[v])
            y_copy(v, g, gx).start()

        return 0

    left = left_ref[...]
    right = right_ref[...]
    base = waves_ref[...]

    def f_copy(q, at, piece, side):
        slot = at * pieces + piece
        return pltpu.make_async_remote_copy(
            src_ref=spec.at[slot, pl.ds((1 - core) * mine, mine)],
            dst_ref=cols.at[q, (at * 2 + side) * pieces + piece],
            send_sem=f_send.at[q * slots + slot], recv_sem=f_recv.at[q * slots + slot],
            device_id=(partner, g), device_id_type=MESH,
        )

    def b_copy(q, at, piece, side):
        slot = at * pieces + piece
        return pltpu.make_async_remote_copy(
            src_ref=cols.at[q, (at * 2 + 1 - side) * pieces + piece],
            dst_ref=back.at[q, slot, pl.ds(side * mine, mine)],
            send_sem=b_send.at[q * slots + slot], recv_sem=b_recv.at[q * slots + slot],
            device_id=(partner, g), device_id_type=MESH,
        )

    order = [(g, 0), (g, 1), (gy, 0), (gx, 0), (gy, 1), (gx, 1), (gd, 0), (gd, 1)]

    def forward(q, i):
        at = pick(i, [a for a, _ in order])
        piece = pick(i, [p for _, p in order])
        far = at == gd

        @pl.when(jnp.logical_or(far, at == gy))
        def _():
            start = q * 2 * half + jnp.where(far, half, 0) + piece * depth

            def arrive(e, _):
                y_copy(start + e, gy, gd).wait_recv()
                return 0

            lax.fori_loop(0, depth, arrive, 0)

        if q == 0:
            @pl.when(far)
            def _():
                for e in range(2):
                    or_copy(2 * piece + e, gd).wait_recv()

        slot = at * pieces + piece
        if q > 0:
            f_copy(q - 1, at, piece, core).wait_send()
        for k in range(0, depth, 2):
            here = pl.ds(piece * depth + k, 2)
            pair = src[q, at, here] * orb[row, at, here]
            rows = along_lanes(pair.reshape(2 * n, n), right)
            planes = along_rows(left, rows[:n], rows[n:])
            spec[slot, pl.ds(k, n, stride=depth), :] = planes[:, :n]
            spec[slot, pl.ds(k + 1, n, stride=depth), :] = planes[:, n:]
        f_copy(q, at, piece, core).start()
        cols[q, (at * 2 + core) * pieces + piece] = spec[slot, pl.ds(core * mine, mine), :]

    def every(q, copy_of):
        for at in range(grids):
            for piece in range(pieces):
                copy_of(q, at, piece)

    lines_count = n // 4

    def lines(q, first, count):
        def line(k):
            held = [
                cols[q, :, pl.ds(pl.multiple_of((2 * k + e) * depth, depth), depth), :].reshape(n, n)
                for e in range(2)
            ]
            moved = along_rows(left, held[0], held[1])
            filtered = []
            for e in range(2):
                ky = core * (n // 2) + 2 * k + e
                signed = jnp.where(ky < n // 2, ky, ky - n).astype(jnp.float32)
                wave = signed * (2.0 * math.pi / n)
                filtered.append(moved[:, e * n:(e + 1) * n] * (volume / (base + wave * wave)))
            done = along_rows(left, filtered[0], filtered[1])
            for e in range(2):
                cols[q, :, pl.ds(pl.multiple_of((2 * k + e) * depth, depth), depth), :] = (
                    done[:, e * n:(e + 1) * n].reshape(n // depth, depth, n)
                )

        def group(i, _):
            for e in range(2):
                line(first + 2 * i + e)
            return 0

        lax.fori_loop(0, count // 2, group, 0)

    def inverse(q, at, piece):
        slot = at * pieces + piece
        b_copy(q, at, piece, 1 - core).wait_recv()
        back[q, slot, pl.ds(core * mine, mine), :] = cols[q, (at * 2 + core) * pieces + piece]
        for k in range(0, depth, 2):
            planes = along_rows(
                left,
                back[q, slot, pl.ds(k, n, stride=depth), :],
                back[q, slot, pl.ds(k + 1, n, stride=depth), :],
            )
            rows = jnp.concatenate([planes[:, :n], planes[:, n:]], axis=0)
            potential = along_lanes(rows, right).reshape(2, n, n)
            here = pl.ds(piece * depth + k, 2)
            value = src[q, at, here] * potential
            if q == 0:
                terms[at, here] = value
            else:
                terms[at, here] += value

    def p_copy(at, side, m):
        return pltpu.make_async_remote_copy(
            src_ref=terms.at[at, pl.ds(m * pair, pair)],
            dst_ref=pin.at[side, pl.ds(m * pair, pair)],
            send_sem=p_send.at[side * pairs + m], recv_sem=p_recv.at[side * pairs + m],
            device_id=(b, gx), device_id_type=MESH,
        )

    def bounds(q, remote):
        local = [q * 2 * half + lag + side * half + (p + 1) * depth for side in range(2) for p in range(2)]
        far = [at + remote for at in local]
        last = [far[2] + 6, far[3] + 1] if q == 0 else far[2:]
        return [local[0], local[1], far[0], local[2], far[1], local[3], *last]

    first_bounds = bounds(0, 10)
    second_bounds = bounds(1, 10)

    def advance(start, stop):
        lax.fori_loop(start, stop, step, 0)

    def first_forward(i, at):
        stop = pick(i, first_bounds)
        advance(at, stop)
        forward(0, i)
        return stop

    at = lax.fori_loop(0, slots, first_forward, 0)
    advance(first_bounds[-1], first_bounds[-1] + 2)
    every(0, lambda q, at, piece: f_copy(q, at, piece, 1 - core).wait_recv())
    settle = first_bounds[-1] + 2

    def first_lines(i, _):
        lines(0, i * (lines_count // slots), lines_count // slots)
        advance(settle + i, settle + i + 1)
        return 0

    lax.fori_loop(0, slots, first_lines, 0)
    every(0, lambda q, at, piece: b_copy(q, at, piece, core).start())
    reached = settle + slots

    def second_forward(i, at):
        stop = jnp.maximum(pick(i, second_bounds), reached + 2 * (i + 1))
        middle = jnp.minimum(at + 1, stop)
        advance(at, middle)
        inverse(0, lax.div(i, pieces), lax.rem(i, pieces))
        advance(middle, stop)
        forward(1, i)

        for d in range(1, bands):
            target = lax.rem(b + d, bands)
            nearer = lax.div(target, 2) == jnp.where(z < nz // 2, nz // 2, nz // 2 - 1)

            @pl.when(i == jnp.where(nearer, 4, 5))
            def _():
                o_copy(target, b, 1).start()

        return stop

    lax.fori_loop(0, slots, second_forward, reached)
    every(1, lambda q, at, piece: f_copy(q, at, piece, 1 - core).wait_recv())
    lines(1, 0, lines_count)
    for at in (gd, gx, gy, g):
        for piece in range(pieces):
            b_copy(1, at, piece, core).start()

    fcol[b] = own[:, pl.ds(b * yb, yb), :]
    part[...] = jnp.zeros_like(part)

    def second_inverse(i, _):
        at = pick(lax.div(i, pieces), [gd, gx, gy, g])
        piece = lax.rem(i, pieces)
        inverse(1, at, piece)

        @pl.when(i < 2 * pieces)
        def _():
            for e in range(depth // pair):
                p_copy(at, lax.div(i, pieces), depth // pair * piece + e).start()

        return 0

    lax.fori_loop(0, slots, second_inverse, 0)

    orbital = 2 * z + row

    wait = 3
    def t_copy(m, at, target):
        rows = pl.ds(m * pair, pair)
        return pltpu.make_async_remote_copy(
            src_ref=terms.at[at, rows, pl.ds(target * yb, yb)],
            dst_ref=tcol.at[orbital, pl.ds(core * half + m * pair, pair)],
            send_sem=t_send.at[(jnp.where(at == g, 1, 0) * pairs + m) * bands + target],
            recv_sem=t_recv.at[(orbital * 2 + core) * pairs + m],
            device_id=(target, at), device_id_type=MESH,
        )

    def t_arrival(m, which, side):
        block = tcol.at[which, pl.ds(side * half + m * pair, pair)]
        return pltpu.make_async_remote_copy(
            src_ref=block, dst_ref=block,
            send_sem=t_send.at[0], recv_sem=t_recv.at[(which * 2 + side) * pairs + m],
            device_id=(partner, g), device_id_type=MESH,
        )

    def finish(i, _):
        @pl.when(i < 2 * pairs)
        def _():
            own_side = lax.div(i, pairs)
            m = lax.rem(i, pairs)
            at = jnp.where(own_side == 0, gy, g)
            rows = pl.ds(m * pair, pair)
            p_copy(at, own_side, m).wait_recv()
            terms[at, rows] += pin[own_side, rows]

            @pl.when(own_side == 0)
            def _():
                for target in range(bands):
                    t_copy(m, gy, target).start()

            @pl.when(own_side == 1)
            def _():
                for d in range(1, bands):
                    t_copy(m, g, lax.rem(b + d, bands)).start()
                tcol[orbital, pl.ds(core * half + m * pair, pair)] = terms[
                    g, rows, pl.ds(b * yb, yb), :
                ]

        @pl.when(i == wait)
        def _():
            for d in range(1, bands):
                for late in range(2):
                    o_copy(b, lax.rem(b + d, bands), late).wait_recv()

        @pl.when(i >= wait)
        def _():
            own_side = lax.div(i - wait, pairs)
            m = lax.rem(i - wait, pairs)
            parity = jnp.where(own_side == 0, 1 - row, row)
            for k in range(nz):
                for side in range(2):
                    local = jnp.logical_and(
                        jnp.logical_and(own_side == 1, z == k), core == side
                    )

                    @pl.when(jnp.logical_not(local))
                    def _():
                        t_arrival(m, 2 * k + parity, side).wait_recv()

            def one(a, _):
                held = [fcol[a, pl.ds(side * half + m * pair, pair)] for side in range(2)]
                for k in range(nz):
                    which = 2 * k + parity
                    total = jnp.zeros((8, n), jnp.float32)
                    for side in range(2):
                        prod = held[side] * tcol[which, pl.ds(side * half + m * pair, pair)]
                        total = total + jnp.sum(prod.reshape(-1, 8, n), axis=0)
                    part[a * bands + which] += total
                return 0

            lax.fori_loop(0, bands, one, 0)

        return 0

    lax.fori_loop(0, 2 * pairs + wait, finish, 0)

    count = bands * bands
    flat = jnp.sum(part[...], axis=1)
    if count < n:
        flat = jnp.concatenate([flat, jnp.zeros((n - count, n), jnp.float32)], axis=0)
    lanes = jnp.sum(flat.T, axis=0, keepdims=True)
    sums_b[b] = jnp.broadcast_to(lanes, (8, n))

    def sb_copy(target, owner):
        return pltpu.make_async_remote_copy(
            src_ref=sums_b.at[b], dst_ref=sums_b.at[owner],
            send_sem=sb_send.at[target], recv_sem=sb_recv.at[owner],
            device_id=(target, g), device_id_type=MESH,
        )

    def sg_copy(target, owner):
        return pltpu.make_async_remote_copy(
            src_ref=sums_g.at[g], dst_ref=sums_g.at[owner],
            send_sem=sg_send.at[target], recv_sem=sg_recv.at[owner],
            device_id=(b, target), device_id_type=MESH,
        )

    for d in range(1, bands):
        sb_copy(lax.rem(b + d, bands), b).start()
    for d in range(1, bands):
        sb_copy(b, lax.rem(b + d, bands)).wait_recv()
    sums_g[g] = jnp.sum(sums_b[...], axis=0)
    for d in range(1, grids):
        sg_copy(lax.rem(g + d, grids), g).start()
    for d in range(1, grids):
        sg_copy(g, lax.rem(g + d, grids)).wait_recv()
    total = jnp.sum(sums_g[...], axis=0)[:1] * volume
    splat[...] = jnp.broadcast_to(total, (n, n)).T

    def entry(i, k):
        first = splat[pl.ds(i * bands + k, 1), :]
        return 0.5 * (first + splat[pl.ds(k * bands + i, 1), :])

    factor = {}
    inverse_diag = {}
    for k in range(bands):
        diag = entry(k, k)
        for m in range(k):
            diag = diag - factor[k, m] * factor[k, m]
        inverse_diag[k] = 1.0 / jnp.sqrt(diag)
        for i in range(k + 1, bands):
            value = entry(i, k)
            for m in range(k):
                value = value - factor[i, m] * factor[k, m]
            factor[i, k] = value * inverse_diag[k]
    for k in range(bands):
        splat[pl.ds(k * bands + k, 1), :] = inverse_diag[k]
        for i in range(k + 1, bands):
            splat[pl.ds(i * bands + k, 1), :] = factor[i, k]

    def leave(p):
        x = pl.ds(4 * p, 4)
        return pltpu.make_async_copy(held_out.at[:, x], out.at[:, x], out_sem.at[p])

    def solve(p, _):
        x = pl.ds(4 * p, 4)
        solved = []
        for i in range(bands):
            value = -tcol[i, x]
            for k in range(i):
                value = value - splat[pl.ds(i * bands + k, 1), :] * solved[k]
            value = value * splat[pl.ds(i * bands + i, 1), :]
            held_out[i, x] = value
            solved.append(value)
        leave(p).start()
        return 0

    lax.fori_loop(0, slab // 4, solve, 0)

    for p in range(slab // 4):
        leave(p).wait()
    for u in range(4):
        mate_copy(u, core).wait_send()
        oy_copy(u, 1 - row, g).wait_send()
        or_copy(u, gy).wait_send()
        for which in range(2):
            ox_copy(u, which, g).wait_send()

    def settle_units(v, _):
        @pl.when(z < nz - 1)
        def _():
            up_copy(v).wait_send()

        @pl.when(z > 0)
        def _():
            dn_copy(v).wait_send()

        y_copy(v, g, gx).wait_send()
        return 0

    lax.fori_loop(0, total_units, settle_units, 0)
    every(phases - 1, lambda q, at, piece: f_copy(q, at, piece, core).wait_send())
    for q in range(phases):
        every(q, lambda q, at, piece: b_copy(q, at, piece, core).wait_send())
    for m in range(pairs):
        p_copy(gd, 0, m).wait_send()
        p_copy(gx, 1, m).wait_send()
        for target in range(bands):
            t_copy(m, gy, target).wait_send()
        for d in range(1, bands):
            t_copy(m, g, lax.rem(b + d, bands)).wait_send()
    for d in range(1, bands):
        for late in range(2):
            o_copy(lax.rem(b + d, bands), b, late).wait_send()
        sb_copy(lax.rem(b + d, bands), b).wait_send()
    for d in range(1, grids):
        sg_copy(lax.rem(g + d, grids), g).wait_send()


def fused(bands, grids, orbitals, sources):
    n = orbitals.shape[2]
    rounds = sources.shape[0]
    slab = n // grids
    half = slab // 2
    depth = 8
    pieces = half // depth
    slots = grids * pieces
    phases = rounds // 2
    yb = n // bands
    numbers = np.arange(n)
    angles = (numbers[:, None] * numbers[None, :] % n) * (2.0 * math.pi / n)
    table = jnp.asarray(np.cos(angles) + np.sin(angles), jnp.float32)
    high, low = parts_of(table)
    left = jnp.block([[high, high], [low, low]])
    right = jnp.block([[high, low], [high, low]])
    signed = np.where(numbers < n // 2, numbers, numbers - n) * (2.0 * math.pi / n)
    screen = (4.0 * math.pi / n) ** 2
    waves = jnp.asarray(signed[:, None] ** 2 + signed[None, :] ** 2 + screen, jnp.float32)
    volume = 1.0 / n**3
    f32 = jnp.float32
    dma = pltpu.SemaphoreType.DMA
    relay = phases * 2 * half
    scratch = [
        pltpu.VMEM((slab, n, n), f32),
        pltpu.VMEM((2, grids, half, n, n), f32),
        pltpu.VMEM((relay, n, n), f32),
        pltpu.VMEM((relay, n, n), f32),
        pltpu.VMEM((phases, grids, half, n, n), f32),
        pltpu.VMEM((bands, slab, yb, n), f32),
        pltpu.VMEM((slots, n * depth, n), f32),
        pltpu.VMEM((phases, n // depth, n // 2 * depth, n), f32),
        pltpu.VMEM((phases, slots, n * depth, n), f32),
        pltpu.VMEM((grids, half, n, n), f32),
        pltpu.VMEM((2, half, n, n), f32),
        pltpu.VMEM((bands, slab, yb, n), f32),
        pltpu.VMEM((bands, slab, yb, n), f32),
        pltpu.VMEM((bands * bands, 8, n), f32),
        pltpu.VMEM((bands, 8, n), f32),
        pltpu.VMEM((grids, 8, n), f32),
        pltpu.VMEM((n, n), f32),
        dma((3,)),
        dma((4,)), dma((4,)),
        dma((8,)), dma((8,)),
        dma((4,)), dma((4,)),
        dma((4,)), dma((4,)),
        dma((relay,)), dma((relay,)),
        dma((relay,)), dma((relay,)),
        dma((relay,)), dma((relay,)),
        dma((2 * bands,)), dma((2 * bands,)),
        dma((phases * slots,)), dma((phases * slots,)),
        dma((phases * slots,)), dma((phases * slots,)),
        dma((half,)), dma((half,)),
        dma((half * bands,)), dma((half * bands,)),
        dma((bands,)), dma((bands,)),
        dma((grids,)), dma((grids,)),
        dma((slab // 4,)),
    ]
    vmem = pl.BlockSpec(memory_space=pltpu.VMEM)
    return pl.pallas_call(
        functools.partial(whole_kernel, bands, grids, rounds, 3, slab // 2, depth, n, volume),
        out_shape=jax.ShapeDtypeStruct((bands, slab, yb, n), f32),
        in_specs=[
            pl.BlockSpec(memory_space=pltpu.SMEM),
            pl.BlockSpec(memory_space=pl.ANY),
            vmem, vmem, vmem,
        ],
        out_specs=pl.BlockSpec(memory_space=pl.ANY),
        scratch_shapes=scratch,
        compiler_params=pltpu.CompilerParams(
            collective_id=0, has_side_effects=True, vmem_limit_bytes=63 * 1024 * 1024
        ),
        name="exchange",
    )(sources, orbitals, left, right, waves)


def per_device(orbitals, sources):
    held, slab, full_y, full_z = orbitals.shape
    bands = lax.axis_size("band")
    grids = lax.axis_size("grid")
    n = full_y
    rounds = sources.shape[0]
    fits = (
        held == 1 and n == full_z == slab * grids and n % 128 == 0 and slab % 32 == 0
        and grids == 4 and rounds == grids and bands % 2 == 0 and bands * bands <= n
        and n % (8 * bands) == 0 and 4 * n * n * slab * 29 <= 60 * 2**20
    )
    if fits:
        return fused(bands, grids, orbitals, sources)
    return general(orbitals, sources)


def solution(mesh):
    placed = (P("band", "grid", None, None), P())
    return jax.shard_map(
        per_device,
        mesh=mesh,
        in_specs=placed,
        out_specs=P(None, "grid", "band", None),
        check_vma=False,
    )
```

```python
import functools
import math

import jax
import jax.numpy as jnp
import numpy as np
from jax import lax
from jax.experimental import pallas as pl
from jax.experimental.pallas import tpu as pltpu
from jax.sharding import PartitionSpec as P

highest = lax.Precision.HIGHEST
MESH = pl.DeviceIdType.MESH


def spread_2(block, axis, owner):
    block = jnp.where(lax.axis_index(axis) == owner, block, jnp.zeros_like(block))
    return lax.psum(block, axis)


def cas_table(length):
    index_values = jnp.arange(length, dtype=jnp.int32)
    products = index_values[:, None] * index_values[None, :] % length
    angles = products.astype(jnp.float32) * (2.0 * math.pi / length)
    return jnp.cos(angles) + jnp.sin(angles)


def squared_waves(start, count, length):
    index_values = start + jnp.arange(count, dtype=jnp.int32)
    signed = jnp.where(index_values < length // 2, index_values, index_values - length)
    waves = signed.astype(jnp.float32) * (2.0 * math.pi / length)
    return waves * waves


def general(orbitals, sources):
    band_count, slab_x, full_y, full_z = orbitals.shape
    grid_count = lax.axis_size("grid")
    full_x = slab_x * grid_count
    total_bands = band_count * lax.axis_size("band")
    round_count = sources.shape[0]
    table_x = cas_table(full_x)
    table_y = cas_table(full_y)
    table_z = cas_table(full_z)
    column_y = full_y // grid_count
    start_y = lax.axis_index("grid") * column_y
    waves = (
        squared_waves(0, full_x, full_x)[:, None, None]
        + squared_waves(start_y, column_y, full_y)[None, :, None]
        + squared_waves(0, full_z, full_z)[None, None, :]
    )
    screen = (4.0 * math.pi / full_x) ** 2
    volume = 1.0 / (full_x * full_y * full_z)
    kernel = volume / (waves + screen)

    def plane_transform(field):
        spread = jnp.einsum("bxyz,zk->bxyk", field, table_z, precision=highest)
        return jnp.einsum("bxyk,yj->bxjk", spread, table_y, precision=highest)

    def own_slab(number):
        owner = number // band_count
        local = number % band_count
        return (owner, lax.dynamic_index_in_dim(orbitals, local, 0, keepdims=False))

    def fetch(number):
        owner, slab = own_slab(number)
        return spread_2(slab, "band", owner)

    arrived = [fetch(sources[turn]) for turn in range(round_count)]
    terms = jnp.zeros(orbitals.shape, jnp.float32)
    for turn in range(round_count):
        source = arrived[turn][None]
        spectra = plane_transform(orbitals * source)
        potential_columns = lax.all_to_all(spectra, "grid", split_axis=2, concat_axis=1, tiled=True)
        line_spread = jnp.einsum("bxyz,xa->bayz", potential_columns, table_x, precision=highest)
        line_spread = line_spread * kernel[None]
        filtered = jnp.einsum("bayz,ax->bxyz", line_spread, table_x, precision=highest)
        terms = terms + source * plane_transform(
            lax.all_to_all(filtered, "grid", split_axis=1, concat_axis=2, tiled=True)
        )
    orbital_cols, term_cols = (
        lax.all_to_all(orbitals, "band", split_axis=2, concat_axis=0, tiled=True),
        lax.all_to_all(terms, "band", split_axis=2, concat_axis=0, tiled=True),
    )
    flat_orbitals = orbital_cols.reshape(total_bands, -1)
    flat_terms = term_cols.reshape(total_bands, -1)
    partial_intersection = (
        jnp.dot(flat_orbitals, flat_terms.T, precision=highest, preferred_element_type=jnp.float32)
        * volume
    )
    intersection = lax.psum(partial_intersection, ("band", "grid"))
    factor = jnp.linalg.cholesky(intersection)
    solved = lax.linalg.triangular_solve(factor, flat_terms, left_side=True, lower=True)
    return (-solved).reshape(term_cols.shape)


def parts_of(value):
    high = value.astype(jnp.bfloat16)
    low = (value - high.astype(jnp.float32)).astype(jnp.bfloat16)
    return high, low


def along_rows(left, first, second):
    n = first.shape[0]
    h0, l0 = parts_of(first)
    h1, l1 = parts_of(second)
    right = jnp.concatenate(
        [jnp.concatenate([h0, h1], axis=1), jnp.concatenate([l0, l1], axis=1)], axis=0
    )
    both = jnp.dot(left, right, preferred_element_type=jnp.float32)
    return both[:n] + both[n:]


def along_lanes(rows, right):
    n = rows.shape[1]
    high, low = parts_of(rows)
    both = jnp.dot(
        jnp.concatenate([high, low], axis=1), right, preferred_element_type=jnp.float32
    )
    return both[:, :n] + both[:, n:]


def pick(i, values):
    out = values[-1]
    for m in reversed(range(len(values) - 1)):
        out = jnp.where(i == m, values[m], out)
    return out


def whole_kernel(
    bands, grids, rounds, ahead, early, depth, n, volume,
    sources, orbitals, left_ref, right_ref, waves_ref, out, *scratch,
):
    (own, orb, up, dn, src, fcol, spec, cols, back, terms, pin, tcol, held_out, part, sums_b, sums_g, splat,
     in_sem, m_send, m_recv, ox_send, ox_recv, oy_send, oy_recv, or_send, or_recv,
     up_send, up_recv, dn_send, dn_recv, y_send, y_recv, o_send, o_recv, f_send, f_recv,
     b_send, b_recv, p_send, p_recv, t_send, t_recv,
     sb_send, sb_recv, sg_send, sg_recv, out_sem) = scratch
    b = lax.axis_index("band")
    g = lax.axis_index("grid")
    nz = bands // 2
    z, core = b // 2, b % 2
    slab = n // grids
    half = slab // 2
    yb = n // bands
    pieces = half // depth
    slots = grids * pieces
    quarter = half // 4
    pair = 2
    pairs = half // pair
    mine = n // 2 * depth
    phases = rounds // 2
    total_units = phases * 2 * half
    lag = (nz - 1) * ahead
    partner = z * 2 + (1 - core)
    gx = g + 1 - 2 * (g % 2)
    gy = lax.rem(g + 2, grids)
    gd = gx + 2 - 4 * (gx // 2)
    column, row = g % 2, g // 2

    barrier = pltpu.get_barrier_semaphore()
    for d in range(1, bands):
        pl.semaphore_signal(barrier, inc=1, device_id=(lax.rem(b + d, bands), g), device_id_type=MESH)
    for d in range(bands):
        pl.semaphore_signal(barrier, inc=1, device_id=(lax.rem(b + d, bands), gy), device_id_type=MESH)
    pl.semaphore_signal(barrier, inc=1, device_id=(b, gx), device_id_type=MESH)
    pl.semaphore_signal(barrier, inc=1, device_id=(b, gd), device_id_type=MESH)
    loads = [
        pltpu.make_async_copy(
            orbitals.at[0, pl.ds((1 - core) * half, half)], own.at[pl.ds((1 - core) * half, half)],
            in_sem.at[0],
        ),
        pltpu.make_async_copy(
            orbitals.at[0, pl.ds(core * half, half)], orb.at[core, g], in_sem.at[1]
        ),
        pltpu.make_async_copy(
            orbitals.at[0, pl.ds(core * half, half)], own.at[pl.ds(core * half, half)], in_sem.at[2]
        ),
    ]
    for load in loads:
        load.start()
    for load in loads:
        load.wait()
    pl.semaphore_wait(barrier, 2 * bands + 1)

    def mate_copy(u, parity):
        return pltpu.make_async_remote_copy(
            src_ref=own.at[pl.ds((1 - core) * half + u * quarter, quarter)],
            dst_ref=orb.at[parity, g, pl.ds(u * quarter, quarter)],
            send_sem=m_send.at[u], recv_sem=m_recv.at[u],
            device_id=(partner, g), device_id_type=MESH,
        )

    def ox_copy(u, which, owner):
        block = orb.at[which, owner, pl.ds(u * quarter, quarter)]
        return pltpu.make_async_remote_copy(
            src_ref=block, dst_ref=block,
            send_sem=ox_send.at[2 * u + which], recv_sem=ox_recv.at[2 * u + which],
            device_id=(b, gx), device_id_type=MESH,
        )

    def oy_copy(u, which, owner):
        block = orb.at[which, owner, pl.ds(u * quarter, quarter)]
        return pltpu.make_async_remote_copy(
            src_ref=block, dst_ref=block,
            send_sem=oy_send.at[u], recv_sem=oy_recv.at[u],
            device_id=(b, gy), device_id_type=MESH,
        )

    def or_copy(u, owner):
        block = orb.at[row, owner, pl.ds(u * quarter, quarter)]
        return pltpu.make_async_remote_copy(
            src_ref=block, dst_ref=block,
            send_sem=or_send.at[u], recv_sem=or_recv.at[u],
            device_id=(b, gx), device_id_type=MESH,
        )

    def up_copy(v):
        return pltpu.make_async_remote_copy(
            src_ref=up.at[v], dst_ref=up.at[v],
            send_sem=up_send.at[v], recv_sem=up_recv.at[v],
            device_id=(lax.rem(b + 2, bands), g), device_id_type=MESH,
        )

    def dn_copy(v):
        return pltpu.make_async_remote_copy(
            src_ref=dn.at[v], dst_ref=dn.at[v],
            send_sem=dn_send.at[v], recv_sem=dn_recv.at[v],
            device_id=(lax.rem(b + bands - 2, bands), g), device_id_type=MESH,
        )

    def place(v):
        q = lax.div(v, 2 * half)
        side = lax.rem(lax.div(v, half), 2)
        return q, side, lax.rem(v, half)

    def y_copy(v, near, far):
        q, side, u = place(v)
        block = src.at[q, jnp.where(side == 0, near, far), u]
        return pltpu.make_async_remote_copy(
            src_ref=block, dst_ref=block,
            send_sem=y_send.at[v], recv_sem=y_recv.at[v],
            device_id=(b, gy), device_id_type=MESH,
        )

    def o_copy(target, owner, late):
        planes = pl.ds(early, slab - early) if late else pl.ds(0, early)
        return pltpu.make_async_remote_copy(
            src_ref=own.at[planes, pl.ds(target * yb, yb)], dst_ref=fcol.at[owner, planes],
            send_sem=o_send.at[late * bands + target], recv_sem=o_recv.at[late * bands + owner],
            device_id=(target, g), device_id_type=MESH,
        )

    for u in range(4):
        mate_copy(u, core).start()
    for d in range(1, bands):
        o_copy(lax.rem(b + d, bands), b, 0).start()
    for u in range(4):
        mate_copy(u, 1 - core).wait_recv()
        oy_copy(u, 1 - row, g).start()
        for which in range(2):
            ox_copy(u, which, g).start()

    def step(t, _):
        @pl.when(jnp.logical_and(t >= half, jnp.logical_and(t < 2 * half, lax.rem(t, quarter) == 0)))
        def _():
            u = lax.div(t - half, quarter)
            for which in range(2):
                ox_copy(u, which, gx).wait_recv()

        for u in range(4):
            @pl.when(t == quarter * (u + 1) + 3)
            def _():
                oy_copy(u, row, gy).wait_recv()
                or_copy(u, gy).start()

        def pass_on(v, box, copy, first, last):
            @pl.when(jnp.logical_and(v >= 0, v < total_units))
            def _():
                q, side, u = place(v)
                s = sources[phases * column + q]
                at = jnp.where(side == 0, g, gx)
                here = jnp.where(lax.rem(s, 2) == 0, orb[0, at, u], orb[1, at, u])

                @pl.when(first)
                def _():
                    box[v] = here

                @pl.when(jnp.logical_not(first))
                def _():
                    copy(v).wait_recv()
                    box[v] = jnp.where(lax.div(s, 2) == z, here, box[v])

                @pl.when(jnp.logical_not(last))
                def _():
                    copy(v).start()

        pass_on(t - z * ahead, up, up_copy, z == 0, z == nz - 1)
        pass_on(t - (nz - 1 - z) * ahead, dn, dn_copy, z == nz - 1, z == 0)
        v = t - lag

        @pl.when(jnp.logical_and(v >= 0, v < total_units))
        def _():
            q, side, u = place(v)
            s = sources[phases * column + q]
            src[q, jnp.where(side == 0, g, gx), u] = jnp.where(s < 2 * z + 2, up[v], dn[v])
            y_copy(v, g, gx).start()

        return 0

    left = left_ref[...]
    right = right_ref[...]
    base = waves_ref[...]

    def f_copy(q, at, piece, side):
        slot = at * pieces + piece
        return pltpu.make_async_remote_copy(
            src_ref=spec.at[slot, pl.ds((1 - core) * mine, mine)],
            dst_ref=cols.at[q, (at * 2 + side) * pieces + piece],
            send_sem=f_send.at[q * slots + slot], recv_sem=f_recv.at[q * slots + slot],
            device_id=(partner, g), device_id_type=MESH,
        )

    def b_copy(q, at, piece, side):
        slot = at * pieces + piece
        return pltpu.make_async_remote_copy(
            src_ref=cols.at[q, (at * 2 + 1 - side) * pieces + piece],
            dst_ref=back.at[q, slot, pl.ds(side * mine, mine)],
            send_sem=b_send.at[q * slots + slot], recv_sem=b_recv.at[q * slots + slot],
            device_id=(partner, g), device_id_type=MESH,
        )

    order = [(g, 0), (g, 1), (gy, 0), (gx, 0), (gy, 1), (gx, 1), (gd, 0), (gd, 1)]

    def forward(q, i):
        at = pick(i, [a for a, _ in order])
        piece = pick(i, [p for _, p in order])
        far = at == gd

        @pl.when(jnp.logical_or(far, at == gy))
        def _():
            start = q * 2 * half + jnp.where(far, half, 0) + piece * depth

            def arrive(e, _):
                y_copy(start + e, gy, gd).wait_recv()
                return 0

            lax.fori_loop(0, depth, arrive, 0)

        if q == 0:
            @pl.when(far)
            def _():
                for e in range(2):
                    or_copy(2 * piece + e, gd).wait_recv()

        slot = at * pieces + piece
        if q > 0:
            f_copy(q - 1, at, piece, core).wait_send()
        for k in range(0, depth, 2):
            here = pl.ds(piece * depth + k, 2)
            pair = src[q, at, here] * orb[row, at, here]
            rows = along_lanes(pair.reshape(2 * n, n), right)
            planes = along_rows(left, rows[:n], rows[n:])
            spec[slot, pl.ds(k, n, stride=depth), :] = planes[:, :n]
            spec[slot, pl.ds(k + 1, n, stride=depth), :] = planes[:, n:]
        f_copy(q, at, piece, core).start()
        cols[q, (at * 2 + core) * pieces + piece] = spec[slot, pl.ds(core * mine, mine), :]

    def every(q, copy_of):
        for at in range(grids):
            for piece in range(pieces):
                copy_of(q, at, piece)

    lines_count = n // 4

    def lines(q, first, count):
        def line(k):
            held = [
                cols[q, :, pl.ds(pl.multiple_of((2 * k + e) * depth, depth), depth), :].reshape(n, n)
                for e in range(2)
            ]
            moved = along_rows(left, held[0], held[1])
            filtered = []
            for e in range(2):
                ky = core * (n // 2) + 2 * k + e
                signed = jnp.where(ky < n // 2, ky, ky - n).astype(jnp.float32)
                wave = signed * (2.0 * math.pi / n)
                filtered.append(moved[:, e * n:(e + 1) * n] * (volume / (base + wave * wave)))
            done = along_rows(left, filtered[0], filtered[1])
            for e in range(2):
                cols[q, :, pl.ds(pl.multiple_of((2 * k + e) * depth, depth), depth), :] = (
                    done[:, e * n:(e + 1) * n].reshape(n // depth, depth, n)
                )

        def group(i, _):
            for e in range(2):
                line(first + 2 * i + e)
            return 0

        lax.fori_loop(0, count // 2, group, 0)

    def inverse(q, at, piece):
        slot = at * pieces + piece
        b_copy(q, at, piece, 1 - core).wait_recv()
        back[q, slot, pl.ds(core * mine, mine), :] = cols[q, (at * 2 + core) * pieces + piece]
        for k in range(0, depth, 2):
            planes = along_rows(
                left,
                back[q, slot, pl.ds(k, n, stride=depth), :],
                back[q, slot, pl.ds(k + 1, n, stride=depth), :],
            )
            rows = jnp.concatenate([planes[:, :n], planes[:, n:]], axis=0)
            potential = along_lanes(rows, right).reshape(2, n, n)
            here = pl.ds(piece * depth + k, 2)
            value = src[q, at, here] * potential
            if q == 0:
                terms[at, here] = value
            else:
                terms[at, here] += value

    def p_copy(at, side, m):
        return pltpu.make_async_remote_copy(
            src_ref=terms.at[at, pl.ds(m * pair, pair)],
            dst_ref=pin.at[side, pl.ds(m * pair, pair)],
            send_sem=p_send.at[side * pairs + m], recv_sem=p_recv.at[side * pairs + m],
            device_id=(b, gx), device_id_type=MESH,
        )

    def bounds(q, remote):
        local = [q * 2 * half + lag + side * half + (p + 1) * depth for side in range(2) for p in range(2)]
        far = [at + remote for at in local]
        last = [far[2] + 6, far[3] + 1] if q == 0 else far[2:]
        return [local[0], local[1], far[0], local[2], far[1], local[3], *last]

    first_bounds = bounds(0, 10)
    second_bounds = bounds(1, 10)

    def advance(start, stop):
        lax.fori_loop(start, stop, step, 0)

    def first_forward(i, at):
        stop = pick(i, first_bounds)
        advance(at, stop)
        forward(0, i)
        return stop

    at = lax.fori_loop(0, slots, first_forward, 0)
    advance(first_bounds[-1], first_bounds[-1] + 2)
    every(0, lambda q, at, piece: f_copy(q, at, piece, 1 - core).wait_recv())
    settle = first_bounds[-1] + 2

    def first_lines(i, _):
        lines(0, i * (lines_count // slots), lines_count // slots)
        advance(settle + i, settle + i + 1)
        return 0

    lax.fori_loop(0, slots, first_lines, 0)
    every(0, lambda q, at, piece: b_copy(q, at, piece, core).start())
    reached = settle + slots

    def second_forward(i, at):
        stop = jnp.maximum(pick(i, second_bounds), reached + 2 * (i + 1))
        middle = jnp.minimum(at + 1, stop)
        advance(at, middle)
        inverse(0, lax.div(i, pieces), lax.rem(i, pieces))
        advance(middle, stop)
        forward(1, i)

        for d in range(1, bands):
            target = lax.rem(b + d, bands)
            nearer = lax.div(target, 2) == jnp.where(z < nz // 2, nz // 2, nz // 2 - 1)

            @pl.when(i == jnp.where(nearer, 4, 5))
            def _():
                o_copy(target, b, 1).start()

        return stop

    lax.fori_loop(0, slots, second_forward, reached)
    every(1, lambda q, at, piece: f_copy(q, at, piece, 1 - core).wait_recv())
    lines(1, 0, lines_count)
    for at in (gd, gx, gy, g):
        for piece in range(pieces):
            b_copy(1, at, piece, core).start()

    fcol[b] = own[:, pl.ds(b * yb, yb), :]
    part[...] = jnp.zeros_like(part)

    def second_inverse(i, _):
        at = pick(lax.div(i, pieces), [gd, gx, gy, g])
        piece = lax.rem(i, pieces)
        inverse(1, at, piece)

        @pl.when(i < 2 * pieces)
        def _():
            for e in range(depth // pair):
                p_copy(at, lax.div(i, pieces), depth // pair * piece + e).start()

        return 0

    lax.fori_loop(0, slots, second_inverse, 0)

    orbital = 2 * z + row

    wait = 3
    def t_copy(m, at, target):
        rows = pl.ds(m * pair, pair)
        return pltpu.make_async_remote_copy(
            src_ref=terms.at[at, rows, pl.ds(target * yb, yb)],
            dst_ref=tcol.at[orbital, pl.ds(core * half + m * pair, pair)],
            send_sem=t_send.at[(jnp.where(at == g, 1, 0) * pairs + m) * bands + target],
            recv_sem=t_recv.at[(orbital * 2 + core) * pairs + m],
            device_id=(target, at), device_id_type=MESH,
        )

    def t_arrival(m, which, side):
        block = tcol.at[which, pl.ds(side * half + m * pair, pair)]
        return pltpu.make_async_remote_copy(
            src_ref=block, dst_ref=block,
            send_sem=t_send.at[0], recv_sem=t_recv.at[(which * 2 + side) * pairs + m],
            device_id=(partner, g), device_id_type=MESH,
        )

    def finish(i, _):
        @pl.when(i < 2 * pairs)
        def _():
            own_side = lax.div(i, pairs)
            m = lax.rem(i, pairs)
            at = jnp.where(own_side == 0, gy, g)
            rows = pl.ds(m * pair, pair)
            p_copy(at, own_side, m).wait_recv()
            terms[at, rows] += pin[own_side, rows]

            @pl.when(own_side == 0)
            def _():
                for d in range(bands):
                    t_copy(m, gy, lax.rem(b + d, bands)).start()

            @pl.when(own_side == 1)
            def _():
                for d in range(1, bands):
                    t_copy(m, g, lax.rem(b + d, bands)).start()
                tcol[orbital, pl.ds(core * half + m * pair, pair)] = terms[
                    g, rows, pl.ds(b * yb, yb), :
                ]

        @pl.when(i == wait)
        def _():
            for d in range(1, bands):
                for late in range(2):
                    o_copy(b, lax.rem(b + d, bands), late).wait_recv()

        @pl.when(i >= wait)
        def _():
            own_side = lax.div(i - wait, pairs)
            m = lax.rem(i - wait, pairs)
            parity = jnp.where(own_side == 0, 1 - row, row)
            for k in range(nz):
                for side in range(2):
                    local = jnp.logical_and(
                        jnp.logical_and(own_side == 1, z == k), core == side
                    )

                    @pl.when(jnp.logical_not(local))
                    def _():
                        t_arrival(m, 2 * k + parity, side).wait_recv()

            def one(a, _):
                held = [fcol[a, pl.ds(side * half + m * pair, pair)] for side in range(2)]
                for k in range(nz):
                    which = 2 * k + parity
                    total = jnp.zeros((8, n), jnp.float32)
                    for side in range(2):
                        prod = held[side] * tcol[which, pl.ds(side * half + m * pair, pair)]
                        total = total + jnp.sum(prod.reshape(-1, 8, n), axis=0)
                    part[a * bands + which] += total
                return 0

            lax.fori_loop(0, bands, one, 0)

        return 0

    lax.fori_loop(0, 2 * pairs + wait, finish, 0)

    count = bands * bands
    flat = jnp.sum(part[...], axis=1)
    if count < n:
        flat = jnp.concatenate([flat, jnp.zeros((n - count, n), jnp.float32)], axis=0)
    lanes = jnp.sum(flat.T, axis=0, keepdims=True)
    sums_b[b] = jnp.broadcast_to(lanes, (8, n))

    def sb_copy(target, owner):
        return pltpu.make_async_remote_copy(
            src_ref=sums_b.at[b], dst_ref=sums_b.at[owner],
            send_sem=sb_send.at[target], recv_sem=sb_recv.at[owner],
            device_id=(target, g), device_id_type=MESH,
        )

    def sg_copy(target, owner):
        return pltpu.make_async_remote_copy(
            src_ref=sums_g.at[g], dst_ref=sums_g.at[owner],
            send_sem=sg_send.at[target], recv_sem=sg_recv.at[owner],
            device_id=(b, target), device_id_type=MESH,
        )

    for d in range(1, bands):
        sb_copy(lax.rem(b + d, bands), b).start()
    for d in range(1, bands):
        sb_copy(b, lax.rem(b + d, bands)).wait_recv()
    sums_g[g] = jnp.sum(sums_b[...], axis=0)
    for d in range(1, grids):
        sg_copy(lax.rem(g + d, grids), g).start()
    for d in range(1, grids):
        sg_copy(g, lax.rem(g + d, grids)).wait_recv()
    total = jnp.sum(sums_g[...], axis=0)[:1] * volume
    splat[...] = jnp.broadcast_to(total, (n, n)).T

    def entry(i, k):
        first = splat[pl.ds(i * bands + k, 1), :]
        return 0.5 * (first + splat[pl.ds(k * bands + i, 1), :])

    factor = {}
    inverse_diag = {}
    for k in range(bands):
        diag = entry(k, k)
        for m in range(k):
            diag = diag - factor[k, m] * factor[k, m]
        inverse_diag[k] = 1.0 / jnp.sqrt(diag)
        for i in range(k + 1, bands):
            value = entry(i, k)
            for m in range(k):
                value = value - factor[i, m] * factor[k, m]
            factor[i, k] = value * inverse_diag[k]
    for k in range(bands):
        splat[pl.ds(k * bands + k, 1), :] = inverse_diag[k]
        for i in range(k + 1, bands):
            splat[pl.ds(i * bands + k, 1), :] = factor[i, k]

    def leave(p):
        x = pl.ds(4 * p, 4)
        return pltpu.make_async_copy(held_out.at[:, x], out.at[:, x], out_sem.at[p])

    def solve(p, _):
        x = pl.ds(4 * p, 4)
        solved = []
        for i in range(bands):
            value = -tcol[i, x]
            for k in range(i):
                value = value - splat[pl.ds(i * bands + k, 1), :] * solved[k]
            value = value * splat[pl.ds(i * bands + i, 1), :]
            held_out[i, x] = value
            solved.append(value)
        leave(p).start()
        return 0

    lax.fori_loop(0, slab // 4, solve, 0)

    for p in range(slab // 4):
        leave(p).wait()
    for u in range(4):
        mate_copy(u, core).wait_send()
        oy_copy(u, 1 - row, g).wait_send()
        or_copy(u, gy).wait_send()
        for which in range(2):
            ox_copy(u, which, g).wait_send()

    def settle_units(v, _):
        @pl.when(z < nz - 1)
        def _():
            up_copy(v).wait_send()

        @pl.when(z > 0)
        def _():
            dn_copy(v).wait_send()

        y_copy(v, g, gx).wait_send()
        return 0

    lax.fori_loop(0, total_units, settle_units, 0)
    every(phases - 1, lambda q, at, piece: f_copy(q, at, piece, core).wait_send())
    for q in range(phases):
        every(q, lambda q, at, piece: b_copy(q, at, piece, core).wait_send())
    for m in range(pairs):
        p_copy(gd, 0, m).wait_send()
        p_copy(gx, 1, m).wait_send()
        for target in range(bands):
            t_copy(m, gy, target).wait_send()
        for d in range(1, bands):
            t_copy(m, g, lax.rem(b + d, bands)).wait_send()
    for d in range(1, bands):
        for late in range(2):
            o_copy(lax.rem(b + d, bands), b, late).wait_send()
        sb_copy(lax.rem(b + d, bands), b).wait_send()
    for d in range(1, grids):
        sg_copy(lax.rem(g + d, grids), g).wait_send()


def fused(bands, grids, orbitals, sources):
    n = orbitals.shape[2]
    rounds = sources.shape[0]
    slab = n // grids
    half = slab // 2
    depth = 8
    pieces = half // depth
    slots = grids * pieces
    phases = rounds // 2
    yb = n // bands
    numbers = np.arange(n)
    angles = (numbers[:, None] * numbers[None, :] % n) * (2.0 * math.pi / n)
    table = jnp.asarray(np.cos(angles) + np.sin(angles), jnp.float32)
    high, low = parts_of(table)
    left = jnp.block([[high, high], [low, low]])
    right = jnp.block([[high, low], [high, low]])
    signed = np.where(numbers < n // 2, numbers, numbers - n) * (2.0 * math.pi / n)
    screen = (4.0 * math.pi / n) ** 2
    waves = jnp.asarray(signed[:, None] ** 2 + signed[None, :] ** 2 + screen, jnp.float32)
    volume = 1.0 / n**3
    f32 = jnp.float32
    dma = pltpu.SemaphoreType.DMA
    relay = phases * 2 * half
    scratch = [
        pltpu.VMEM((slab, n, n), f32),
        pltpu.VMEM((2, grids, half, n, n), f32),
        pltpu.VMEM((relay, n, n), f32),
        pltpu.VMEM((relay, n, n), f32),
        pltpu.VMEM((phases, grids, half, n, n), f32),
        pltpu.VMEM((bands, slab, yb, n), f32),
        pltpu.VMEM((slots, n * depth, n), f32),
        pltpu.VMEM((phases, n // depth, n // 2 * depth, n), f32),
        pltpu.VMEM((phases, slots, n * depth, n), f32),
        pltpu.VMEM((grids, half, n, n), f32),
        pltpu.VMEM((2, half, n, n), f32),
        pltpu.VMEM((bands, slab, yb, n), f32),
        pltpu.VMEM((bands, slab, yb, n), f32),
        pltpu.VMEM((bands * bands, 8, n), f32),
        pltpu.VMEM((bands, 8, n), f32),
        pltpu.VMEM((grids, 8, n), f32),
        pltpu.VMEM((n, n), f32),
        dma((3,)),
        dma((4,)), dma((4,)),
        dma((8,)), dma((8,)),
        dma((4,)), dma((4,)),
        dma((4,)), dma((4,)),
        dma((relay,)), dma((relay,)),
        dma((relay,)), dma((relay,)),
        dma((relay,)), dma((relay,)),
        dma((2 * bands,)), dma((2 * bands,)),
        dma((phases * slots,)), dma((phases * slots,)),
        dma((phases * slots,)), dma((phases * slots,)),
        dma((half,)), dma((half,)),
        dma((half * bands,)), dma((half * bands,)),
        dma((bands,)), dma((bands,)),
        dma((grids,)), dma((grids,)),
        dma((slab // 4,)),
    ]
    vmem = pl.BlockSpec(memory_space=pltpu.VMEM)
    return pl.pallas_call(
        functools.partial(whole_kernel, bands, grids, rounds, 3, slab // 2, depth, n, volume),
        out_shape=jax.ShapeDtypeStruct((bands, slab, yb, n), f32),
        in_specs=[
            pl.BlockSpec(memory_space=pltpu.SMEM),
            pl.BlockSpec(memory_space=pl.ANY),
            vmem, vmem, vmem,
        ],
        out_specs=pl.BlockSpec(memory_space=pl.ANY),
        scratch_shapes=scratch,
        compiler_params=pltpu.CompilerParams(
            collective_id=0, has_side_effects=True, vmem_limit_bytes=63 * 1024 * 1024
        ),
        name="exchange",
    )(sources, orbitals, left, right, waves)


def per_device(orbitals, sources):
    held, slab, full_y, full_z = orbitals.shape
    bands = lax.axis_size("band")
    grids = lax.axis_size("grid")
    n = full_y
    rounds = sources.shape[0]
    fits = (
        held == 1 and n == full_z == slab * grids and n % 128 == 0 and slab % 32 == 0
        and grids == 4 and rounds == grids and bands % 2 == 0 and bands * bands <= n
        and n % (8 * bands) == 0 and 4 * n * n * slab * 29 <= 60 * 2**20
    )
    if fits:
        return fused(bands, grids, orbitals, sources)
    return general(orbitals, sources)


def solution(mesh):
    placed = (P("band", "grid", None, None), P())
    return jax.shard_map(
        per_device,
        mesh=mesh,
        in_specs=placed,
        out_specs=P(None, "grid", "band", None),
        check_vma=False,
    )
```
